128 devices in a mesh: grp: 8 (over y, z_lo), tp: 16 (over z_hi, x, core).
Axes of the slice: x: 4, y: 4, z: 4 (z_hi: 2, z_lo: 2; z = z_hi * 2 + z_lo), core: 2. Of those that a mesh axis runs over, the one named last changes fastest.
Arguments:
- features: bfloat16 [2048, 49152], P('grp', 'tp'), may hold values from -24 to 24
- weight: bfloat16 [49152, 8192], P('tp', 'grp'), may hold values from -0.049804688 to 0.049804688
- norm_gain: float32 [8192], P('grp'), may hold values from 0.1 to 1.9
- target: bfloat16 [2048, 8192], P(None, 'grp'), may hold values from -6 to 6
- counts: int32 [256], replicated, may hold values from 1 to 8
Outputs:
- weight_grad: bfloat16 [49152, 8192], P('tp', 'grp')
- draft_loss: float32 [], replicated
The draws below stay inside these ranges and needn't reach their ends.
All inputs are finite; a program needn't handle non-finite values.
Results may differ from the reference program's by a relative error of at most 0.0085.
Values may be sent and summed in bfloat16 or wider, within the bound.
A program may use at most 128 MiB of HBM per device.

```python
import math
import jax
import jax.numpy as jnp
from jax import lax

DM = 16384
DOUT = 8192
SPEC = 8
REQ = 32
TOKENS = 2048
N_GRP = 8


def draw_features(key, part):
    first, second, third = jax.random.split(key, 3)
    base = jax.random.normal(first, (TOKENS, 3 * DM), jnp.float32)
    base = jnp.clip(base, -4.0, 4.0)
    row_scale = jnp.exp(jax.random.uniform(second, (TOKENS, 1), jnp.float32, math.log(0.3), math.log(3.0)))
    col_scale = jnp.exp(jax.random.uniform(third, (1, 3 * DM), jnp.float32, math.log(0.5), math.log(2.0)))
    return jnp.clip(base * row_scale * col_scale, -24.0, 24.0).astype(jnp.bfloat16)


def draw_weight(key, part):
    first, second = jax.random.split(key, 2)
    base = jnp.clip(jax.random.normal(first, (3 * DM, DOUT), jnp.float32), -4.0, 4.0)
    col_scale = jnp.exp(jax.random.uniform(second, (1, DOUT), jnp.float32, math.log(0.3), math.log(3.0)))
    return jnp.clip(base * col_scale / math.sqrt(3 * DM), -0.0498046875, 0.0498046875).astype(jnp.bfloat16)


def plant(values, stream_key, least, top_value):
    dims = values.shape
    place = [jax.random.randint(jax.random.fold_in(stream_key, axis), (), 0, dims[axis]) for axis in range(len(dims))]
    values = values.at[tuple(place)].set(least)
    longest = dims.index(max(dims))
    place[longest] = (place[longest] + 1) % dims[longest]
    return values.at[tuple(place)].set(top_value)


def block_levels(rng, extent, pieces, low, largest):
    level, own = 1.0, jax.random.fold_in(rng, 6)
    for position, shards_of in pieces:
        draws = jnp.exp(jax.random.uniform(jax.random.fold_in(own, position), (shards_of,), jnp.float32, low / len(pieces), largest / len(pieces)))
        level = level * jnp.repeat(draws, extent[position] // shards_of).reshape([-1 if axis == position else 1 for axis in range(len(extent))])
    return level


def bell_draw(own_key, shape, scale, most, pieces=(), held_as=jnp.bfloat16):
    result = scale * jax.random.normal(own_key, shape, jnp.float32)
    if pieces:
        result = result * block_levels(own_key, shape, pieces, -0.22, 0.18)
    return jnp.clip(result, -most, most).astype(held_as)


def setup_inputs(seed: int = 0) -> dict:
    streams_of = jax.random.split(jax.random.key(seed), 6)
    return {
        "features": draw_features(jax.random.fold_in(streams_of[5], 71), 0),
        "weight": draw_weight(jax.random.fold_in(streams_of[5], 71), 0),
        "norm_gain": jnp.clip(1.0 + 0.18 * jax.random.normal(streams_of[2], (DOUT,), jnp.float32), 0.1, 1.9),
        "target": bell_draw(streams_of[3], (TOKENS, DOUT), 1.0, 6.0, ((1, 8),)),
        "counts": plant(jax.random.randint(streams_of[4], (N_GRP * REQ,), 1, SPEC + 1), jax.random.fold_in(streams_of[4], 1), 1, SPEC).astype(jnp.int32),
    }


epsilon = 1e-06

def reference(features, weight, norm_gain, target, counts):
    hidden = jnp.dot(features, weight, preferred_element_type=jnp.float32)
    row_index = jnp.arange(TOKENS, dtype=jnp.int32)
    row_live = (row_index % SPEC < jnp.take(counts, row_index // SPEC)).astype(jnp.float32)[:, None]
    accepted = jnp.sum(counts).astype(jnp.float32)
    squares = lax.optimization_barrier(jnp.sum(hidden * hidden, axis=1, keepdims=True))
    inverse_rms = lax.rsqrt(squares / DOUT + epsilon)
    normed = hidden * inverse_rms * norm_gain[None, :]
    deviation = normed - target.astype(jnp.float32)
    residual = row_live * deviation / accepted
    coupling = lax.optimization_barrier(jnp.sum(norm_gain[None, :] * residual * hidden, axis=1, keepdims=True))
    act_grad = (inverse_rms * norm_gain[None, :] * residual - hidden * inverse_rms ** 3 * coupling / DOUT).astype(jnp.bfloat16)
    weight_grad = lax.dot_general(features, act_grad, (((0,), (0,)), ((), ())), preferred_element_type=jnp.float32).astype(jnp.bfloat16)
    draft_loss = 0.5 * jnp.sum(residual * deviation)
    return (weight_grad, draft_loss)
```

```python
import functools

import jax
import jax.numpy as jnp
from jax import lax
from jax.experimental import pallas as pl
from jax.experimental.pallas import tpu as pltpu
from jax.sharding import PartitionSpec as P

SPEC = 8
EPS = 1e-06
CHUNKS = (64, 64, 64, 64)
TILE = 256
MESH = pl.DeviceIdType.MESH

TP_OFF = ((0, 1), (0, 3), (0, 2), (1, 0), (1, 1), (1, 3), (1, 2))
GRP_OFF = ((0, 1), (1, 0), (3, 0), (2, 0), (1, 1), (3, 1), (2, 1))


def kernel(
    dout, split, features, weight, gain_ref, target, counts_s, counts_v, out, loss_out,
    fbuf, wbuf, acc, gbuf, stage, hsend, hrecv, hown, hsum, rsrecv, hid, tgt,
    st_own, st_recv, loss_acc, l1_recv, l2_own, l2_recv,
    w_sem, f_sem, t_sem, o_sem,
    ag_s, ag_r, hp_s, hp_r, rs_s, rs_r, st_s, st_r, ga_s, ga_r, gp_s, gp_r,
    l1_s, l1_r, l2_s, l2_r,
):
    g, t = lax.axis_index("grp"), lax.axis_index("tp")
    y, zl = g // 2, lax.rem(g, 2)
    core, q = lax.rem(t, 2), t // 2
    zh, x = q // 4, lax.rem(q, 4)
    depth, cols = wbuf.shape
    rows_g = features.shape[0]
    n_chunks = len(CHUNKS)
    offs = [sum(CHUNKS[:c]) for c in range(n_chunks)]
    a_cols, a_half, half = split

    def grp_dev(dy, dz):
        return lax.rem(y + dy, 4) * 2 + lax.rem(zl + dz, 2)

    def chip(dz, dx):
        return lax.rem(zh + dz, 2) * 4 + lax.rem(x + dx, 4)

    zp, yp, ym, yo = grp_dev(0, 1), grp_dev(1, 0), grp_dev(3, 0), grp_dev(2, 0)
    zyp, zym, zyo = grp_dev(1, 1), grp_dev(3, 1), grp_dev(2, 1)
    other = t + 1 - 2 * core

    tp_peers = [chip(*o) * 2 + core for o in TP_OFF]
    grp_peers = [grp_dev(*o) for o in GRP_OFF]
    all_tp = tp_peers + [chip(*o) * 2 + 1 - core for o in TP_OFF] + [other]

    barrier = pltpu.get_barrier_semaphore()
    for p in grp_peers:
        pl.semaphore_signal(barrier, inc=1, device_id=(p, t), device_id_type=MESH)
    for p in all_tp:
        pl.semaphore_signal(barrier, inc=1, device_id=(g, p), device_id_type=MESH)

    sends = []

    def remote(src, dst, ssem, rsem, dev):
        cp = pltpu.make_async_remote_copy(
            src_ref=src, dst_ref=dst, send_sem=ssem, recv_sem=rsem, device_id=dev, device_id_type=MESH
        )
        cp.start()
        sends.append(cp)

    def arrived(dst, ssem, rsem):
        pltpu.make_async_remote_copy(
            src_ref=dst, dst_ref=dst, send_sem=ssem, recv_sem=rsem, device_id=(zp, t), device_id_type=MESH
        ).wait_recv()

    local = []
    for c in range(n_chunks):
        r = CHUNKS[c]
        cp = pltpu.make_async_copy(
            features.at[pl.ds(offs[c], r), :],
            fbuf.at[pl.ds(pl.multiple_of(8 * offs[c] + g * r, 16), r), :],
            f_sem.at[c],
        )
        cp.start()
        local.append(cp)
    w_cp = pltpu.make_async_copy(weight, wbuf, w_sem)
    w_cp.start()

    def own_rows(c):
        r = CHUNKS[c]
        return (core * 4 + q // 2) * rows_g + offs[c] + lax.rem(q, 2) * (r // 2)

    t_cps = []
    for c in range(n_chunks):
        r = CHUNKS[c]
        cp = pltpu.make_async_copy(
            target.at[pl.ds(pl.multiple_of(own_rows(c), 16), r // 2), :],
            tgt.at[pl.ds(4 * 0 + offs[c] // 2, r // 2), :],
            t_sem.at[c],
        )
        cp.start()
        t_cps.append(cp)

    pl.semaphore_wait(barrier, len(grp_peers) + len(all_tp))

    def seg(c, who, lo, n):
        r = CHUNKS[c]
        return fbuf.at[pl.ds(pl.multiple_of(8 * offs[c] + who * r, 16), r), pl.ds(lo, n)]

    def ag_put(c, k, who, lo, n, dev):
        remote(seg(c, who, lo, n), seg(c, who, lo, n), ag_s.at[c, k], ag_r.at[c, k], (dev, t))

    def ag_own(c, k, lo, n, dev):
        r = CHUNKS[c]
        remote(
            features.at[pl.ds(offs[c], r), pl.ds(lo, n)], seg(c, g, lo, n),
            ag_s.at[c, k], ag_r.at[c, k], (dev, t),
        )

    def ag_got(c, k, who, lo, n):
        arrived(seg(c, who, lo, n), ag_s.at[c, k], ag_r.at[c, k])

    b_cols = depth - a_cols

    def start(c):
        ag_own(c, 0, 0, a_cols, zp)
        ag_own(c, 1, 0, depth, yp)
        ag_own(c, 2, 0, depth, ym)
        ag_own(c, 3, a_cols, b_cols, zp)

    def round1(c):
        ag_got(c, 0, zp, 0, a_cols)
        ag_put(c, 4, zp, 0, a_cols, yp)
        ag_put(c, 5, zp, 0, a_cols, ym)

    def round2(c):
        ag_got(c, 1, ym, 0, depth)
        ag_put(c, 6, ym, 0, half, yp)
        ag_put(c, 10, ym, a_cols, b_cols, zp)
        ag_got(c, 2, yp, 0, depth)
        ag_put(c, 7, yp, half, depth - half, ym)
        ag_put(c, 11, yp, a_cols, b_cols, zp)

    def round3(c):
        ag_got(c, 4, zym, 0, a_cols)
        ag_put(c, 8, zym, 0, a_half, yp)
        ag_got(c, 5, zyp, 0, a_cols)
        ag_put(c, 9, zyp, a_half, a_cols - a_half, ym)

    def round4(c):
        ag_got(c, 6, yo, 0, half)
        ag_got(c, 7, yo, half, depth - half)
        ag_put(c, 12, yo, a_cols, b_cols, zp)

    def finish(c):
        ag_got(c, 3, zp, a_cols, b_cols)
        ag_got(c, 10, zym, a_cols, b_cols)
        ag_got(c, 11, zyp, a_cols, b_cols)
        ag_got(c, 8, zyo, 0, a_half)
        ag_got(c, 9, zyo, a_half, a_cols - a_half)
        ag_got(c, 12, zyo, a_cols, b_cols)
        local[c].wait()

    def matmul_half(c, which, keep):
        r4 = 4 * CHUNKS[c]
        start_row = pl.multiple_of(8 * offs[c] + which * r4, 16)

        def tile(n, _):
            col = pl.ds(pl.multiple_of(n * TILE, TILE), TILE)
            part = jnp.dot(
                fbuf[pl.ds(start_row, r4), :], wbuf[:, col], preferred_element_type=jnp.float32
            )
            if keep:
                hown[pl.ds(0, r4), col] = part
            else:
                hsend[pl.ds(4 * offs[c], r4), col] = part.astype(jnp.bfloat16)
            return 0

        lax.fori_loop(0, cols // TILE, tile, 0)

    def matmul_other(c):
        matmul_half(c, 1 - core, False)
        rows = pl.ds(4 * offs[c], 4 * CHUNKS[c])
        remote(hsend.at[rows, :], hrecv.at[rows, :], hp_s.at[c], hp_r.at[c], (g, other))

    def matmul_mine(c):
        matmul_half(c, core, True)

    def spread(c):
        r = CHUNKS[c]
        base = 4 * offs[c]
        arrived(hrecv.at[pl.ds(base, 4 * r), :], hp_s.at[c], hp_r.at[c])

        def add(i, _):
            lo = pl.multiple_of(i * 16, 16)
            both = hown[pl.ds(lo, 16), :] + hrecv[pl.ds(base + lo, 16), :].astype(jnp.float32)
            hsum[pl.ds(base + lo, 16), :] = both.astype(jnp.bfloat16)
            return 0

        lax.fori_loop(0, 4 * r // 16, add, 0)
        n = r // 2
        for k, o in enumerate(TP_OFF):
            remote(
                hsum.at[pl.ds(pl.multiple_of(base + chip(*o) * n, 16), n), :],
                rsrecv.at[k, pl.ds(offs[c] // 2, n), :],
                rs_s.at[c, k], rs_r.at[c, k], (g, tp_peers[k]),
            )

    def stats(c):
        n = CHUNKS[c] // 2
        rows = pl.ds(offs[c] // 2, n)
        mine = pl.multiple_of(q * n, 16)
        h = hown[pl.ds(mine, n), :]
        h = h + hrecv[pl.ds(pl.multiple_of(4 * offs[c] + mine, 16), n), :].astype(jnp.float32)
        for k in range(7):
            arrived(rsrecv.at[k, rows, :], rs_s.at[c, k], rs_r.at[c, k])
            h = h + rsrecv[k, rows, :].astype(jnp.float32)
        hid[pl.ds(0, n), :] = h
        t_cps[c].wait()
        gh = gain_ref[...] * h
        s1 = jnp.sum(h * h, axis=1, keepdims=True)
        s2 = jnp.sum(gh * gh, axis=1, keepdims=True)
        s3 = jnp.sum(gh * tgt[rows, :].astype(jnp.float32), axis=1, keepdims=True)
        lane = lax.broadcasted_iota(jnp.int32, (n, 128), 1)
        st_own[rows, :] = jnp.where(lane == 0, s1, jnp.where(lane == 1, s2, s3))
        for k in range(7):
            remote(
                st_own.at[rows, :], st_recv.at[k, rows, :], st_s.at[c, k], st_r.at[c, k], (grp_peers[k], t)
            )

    def gradient(c):
        n = CHUNKS[c] // 2
        rows = pl.ds(offs[c] // 2, n)
        total = st_own[rows, :]
        for k in range(7):
            arrived(st_recv.at[k, rows, :], st_s.at[c, k], st_r.at[c, k])
            total = total + st_recv[k, rows, :]
        s1, s2, s3 = total[:, 0:1], total[:, 1:2], total[:, 2:3]
        inv = lax.rsqrt(s1 / dout + EPS)
        accepted = jnp.sum(counts_v[...].astype(jnp.float32), keepdims=True)
        first = own_rows(c) // SPEC
        sub = lax.broadcasted_iota(jnp.int32, (SPEC, 128), 0)
        live = jnp.concatenate(
            [(sub < counts_s[first + i]).astype(jnp.float32) for i in range(n // SPEC)], axis=0
        )[:, 0:1]
        scale = live / accepted
        gain = gain_ref[...]
        h = hid[pl.ds(0, n), :]
        dev = h * inv * gain - tgt[rows, :].astype(jnp.float32)
        res = scale * dev
        coupling = scale * (inv * s2 - s3)
        grad = inv * gain * res - h * (inv * inv * inv * coupling / dout)
        mine = pl.ds(pl.multiple_of(8 * offs[c] + core * 4 * CHUNKS[c] + q * n, 16), n)
        gbuf[mine, :] = grad.astype(jnp.bfloat16)
        lost = res * dev
        part = loss_acc[...]
        for i in range(n // 8):
            for j in range(cols // 128):
                part = part + lost[8 * i : 8 * i + 8, 128 * j : 128 * j + 128]
        loss_acc[...] = part
        for k in range(7):
            remote(gbuf.at[mine, :], gbuf.at[mine, :], ga_s.at[c, k], ga_r.at[c, k], (g, tp_peers[k]))
        remote(gbuf.at[mine, :], gbuf.at[mine, :], gp_s.at[c, 7], gp_r.at[c, 7], (g, other))

    def grad_rows(c, who_core, who_chip):
        n = CHUNKS[c] // 2
        return gbuf.at[pl.ds(pl.multiple_of(8 * offs[c] + who_core * 4 * CHUNKS[c] + who_chip * n, 16), n), :]

    def pass_on(c):
        for k, (dz, dx) in enumerate(TP_OFF):
            ref = grad_rows(c, core, chip((2 - dz) % 2, (4 - dx) % 4))
            arrived(ref, ga_s.at[c, k], ga_r.at[c, k])
            remote(ref, ref, gp_s.at[c, k], gp_r.at[c, k], (g, other))

    def other_grads(c):
        arrived(grad_rows(c, 1 - core, q), gp_s.at[c, 7], gp_r.at[c, 7])
        for k, (dz, dx) in enumerate(TP_OFF):
            arrived(grad_rows(c, 1 - core, chip((2 - dz) % 2, (4 - dx) % 4)), gp_s.at[c, k], gp_r.at[c, k])

    n_tiles = depth // TILE
    last = n_chunks - 1

    def outer(c, lo, hi):
        rows = pl.ds(8 * offs[c], 8 * CHUNKS[c])

        def tile(i, _):
            k = pl.ds(pl.multiple_of(i * TILE, TILE), TILE)
            for n in range(cols // TILE):
                col = pl.ds(n * TILE, TILE)
                part = lax.dot_general(
                    fbuf[rows, k], gbuf[rows, col], (((0,), (0,)), ((), ())),
                    preferred_element_type=jnp.float32,
                )
                if c > 0:
                    part = part + acc[k, col]
                if c == last:
                    stage[k, col] = part.astype(jnp.bfloat16)
                else:
                    acc[k, col] = part
            if c == last:
                pltpu.make_async_copy(stage.at[k, :], out.at[k, :], o_sem.at[i]).start()
            return 0

        lax.fori_loop(lo, hi, tile, 0)

    loss_acc[...] = jnp.zeros_like(loss_acc)
    start(0)
    round1(0)
    round2(0)
    if n_chunks > 1:
        start(1)
    round3(0)
    round4(0)
    w_cp.wait()
    finish(0)
    for c in range(n_chunks):
        more = c + 1 < n_chunks
        matmul_other(c)
        if more:
            round1(c + 1)
        matmul_mine(c)
        if more:
            round2(c + 1)
            if c + 2 < n_chunks:
                start(c + 2)
        if c > 0:
            pass_on(c - 1)
        spread(c)
        if more:
            round3(c + 1)
        if c > 0:
            other_grads(c - 1)
            outer(c - 1, 0, n_tiles)
        if more:
            round4(c + 1)
        stats(c)
        gradient(c)
        if more:
            finish(c + 1)
    for k, p in enumerate(all_tp):
        remote(loss_acc, l1_recv.at[k], l1_s.at[k], l1_r.at[k], (g, p))
    pass_on(last)
    sum1 = loss_acc[...]
    for k in range(15):
        arrived(l1_recv.at[k], l1_s.at[k], l1_r.at[k])
        sum1 = sum1 + l1_recv[k]
    l2_own[...] = sum1
    for k in range(7):
        remote(l2_own, l2_recv.at[k], l2_s.at[k], l2_r.at[k], (grp_peers[k], t))
    other_grads(last)
    outer(last, 0, n_tiles)
    sum2 = l2_own[...]
    for k in range(7):
        arrived(l2_recv.at[k], l2_s.at[k], l2_r.at[k])
        sum2 = sum2 + l2_recv[k]
    loss_out[0, 0] = 0.5 * jnp.sum(sum2)
    for i in range(n_tiles):
        k = pl.ds(i * TILE, TILE)
        pltpu.make_async_copy(stage.at[k, :], out.at[k, :], o_sem.at[i]).wait()
    for cp in sends:
        cp.wait_send()


def shards(features, weight, norm_gain, target, counts):
    rows_g, depth = features.shape
    cols = weight.shape[1]
    total = target.shape[0]
    n = len(CHUNKS)
    bf, f32 = jnp.bfloat16, jnp.float32
    own = total // 16
    dma = pltpu.SemaphoreType.DMA
    anyspace = pl.BlockSpec(memory_space=pl.ANY)
    vmem = pl.BlockSpec(memory_space=pltpu.VMEM)
    unit = depth // 128
    a_units = unit * 16 // 24
    split = (a_units * 128, (a_units // 2) * 128, (unit // 2) * 128)
    out, loss = pl.pallas_call(
        functools.partial(kernel, cols * lax.axis_size("grp"), split),
        out_shape=(
            jax.ShapeDtypeStruct((depth, cols), bf),
            jax.ShapeDtypeStruct((1, 1), f32),
        ),
        in_specs=[anyspace, anyspace, vmem, anyspace, pl.BlockSpec(memory_space=pltpu.SMEM), vmem],
        out_specs=(anyspace, pl.BlockSpec(memory_space=pltpu.SMEM)),
        scratch_shapes=[
            pltpu.VMEM((total, depth), bf),
            pltpu.VMEM((depth, cols), bf),
            pltpu.VMEM((depth, cols), f32),
            pltpu.VMEM((total, cols), bf),
            pltpu.VMEM((depth, cols), bf),
            pltpu.VMEM((total // 2, cols), bf),
            pltpu.VMEM((total // 2, cols), bf),
            pltpu.VMEM((4 * max(CHUNKS), cols), f32),
            pltpu.VMEM((total // 2, cols), bf),
            pltpu.VMEM((7, own, cols), bf),
            pltpu.VMEM((max(CHUNKS) // 2, cols), f32),
            pltpu.VMEM((own, cols), bf),
            pltpu.VMEM((own, 128), f32),
            pltpu.VMEM((7, own, 128), f32),
            pltpu.VMEM((8, 128), f32),
            pltpu.VMEM((15, 8, 128), f32),
            pltpu.VMEM((8, 128), f32),
            pltpu.VMEM((7, 8, 128), f32),
            dma, dma((n,)), dma((n,)), dma((depth // TILE,)),
            dma((n, 13)), dma((n, 13)), dma((n,)), dma((n,)), dma((n, 7)), dma((n, 7)),
            dma((n, 7)), dma((n, 7)), dma((n, 7)), dma((n, 7)), dma((n, 8)), dma((n, 8)),
            dma((15,)), dma((15,)), dma((7,)), dma((7,)),
        ],
        compiler_params=pltpu.CompilerParams(
            collective_id=0, has_side_effects=True, vmem_limit_bytes=64 * 1024 * 1024 - 65536
        ),
    )(features, weight, norm_gain.reshape(1, cols), target, counts, counts.reshape(2, -1))
    return out, loss[0, 0]


def solution(mesh):
    placed = (P("grp", "tp"), P("tp", "grp"), P("grp"), P(None, "grp"), P())
    return jax.shard_map(
        shards, mesh=mesh, in_specs=placed, out_specs=(P("tp", "grp"), P()), check_vma=False
    )
```

```python
import functools

import jax
import jax.numpy as jnp
from jax import lax
from jax.experimental import pallas as pl
from jax.experimental.pallas import tpu as pltpu
from jax.sharding import PartitionSpec as P

SPEC = 8
EPS = 1e-06
CHUNKS = (64, 64, 64, 64)
TILE = 256
MESH = pl.DeviceIdType.MESH

TP_OFF = ((0, 1), (0, 3), (0, 2), (1, 0), (1, 1), (1, 3), (1, 2))
X_OFF = (1, 3, 2)
GRP_OFF = ((0, 1), (1, 0), (3, 0), (2, 0), (1, 1), (3, 1), (2, 1))


def kernel(
    dout, split, features, weight, gain_ref, target, counts_s, counts_v, out, loss_out,
    fbuf, wbuf, acc, gbuf, stage, hsend, hrecv, hown, hsum, xrecv, zsend, zrecv, hid, tgt,
    st_own, st_recv, loss_acc, l1_recv, l2_own, l2_recv,
    w_sem, f_sem, t_sem, o_sem,
    ag_s, ag_r, hp_s, hp_r, rx_s, rx_r, rz_s, rz_r, st_s, st_r, gz_s, gz_r, gx_s, gx_r, gp_s, gp_r,
    l1_s, l1_r, l2_s, l2_r,
):
    g, t = lax.axis_index("grp"), lax.axis_index("tp")
    y, zl = g // 2, lax.rem(g, 2)
    core, q = lax.rem(t, 2), t // 2
    zh, x = q // 4, lax.rem(q, 4)
    depth, cols = wbuf.shape
    rows_g = features.shape[0]
    n_chunks = len(CHUNKS)
    offs = [sum(CHUNKS[:c]) for c in range(n_chunks)]
    a_cols, a_low, half = split
    a_halves = [a_low if c % 2 == 0 else a_cols - a_low for c in range(n_chunks)]
    place = x * 2 + zh

    def grp_dev(dy, dz):
        return lax.rem(y + dy, 4) * 2 + lax.rem(zl + dz, 2)

    def chip(dz, dx):
        return lax.rem(zh + dz, 2) * 4 + lax.rem(x + dx, 4)

    zp, yp, ym, yo = grp_dev(0, 1), grp_dev(1, 0), grp_dev(3, 0), grp_dev(2, 0)
    zyp, zym, zyo = grp_dev(1, 1), grp_dev(3, 1), grp_dev(2, 1)
    other = t + 1 - 2 * core

    tp_peers = [chip(*o) * 2 + core for o in TP_OFF]
    x_peers, z_peer = tp_peers[:3], tp_peers[3]
    x_of = [lax.rem(x + dx, 4) for dx in X_OFF]
    x_from = [lax.rem(x + 4 - dx, 4) for dx in X_OFF]
    grp_peers = [grp_dev(*o) for o in GRP_OFF]
    all_tp = tp_peers + [chip(*o) * 2 + 1 - core for o in TP_OFF] + [other]

    barrier = pltpu.get_barrier_semaphore()
    for p in grp_peers:
        pl.semaphore_signal(barrier, inc=1, device_id=(p, t), device_id_type=MESH)
    for p in all_tp:
        pl.semaphore_signal(barrier, inc=1, device_id=(g, p), device_id_type=MESH)

    sends = []

    def remote(src, dst, ssem, rsem, dev):
        cp = pltpu.make_async_remote_copy(
            src_ref=src, dst_ref=dst, send_sem=ssem, recv_sem=rsem, device_id=dev, device_id_type=MESH
        )
        cp.start()
        sends.append(cp)

    def arrived(dst, ssem, rsem):
        pltpu.make_async_remote_copy(
            src_ref=dst, dst_ref=dst, send_sem=ssem, recv_sem=rsem, device_id=(zp, t), device_id_type=MESH
        ).wait_recv()

    local = []
    for c in range(n_chunks):
        r = CHUNKS[c]
        cp = pltpu.make_async_copy(
            features.at[pl.ds(offs[c], r), :],
            fbuf.at[pl.ds(pl.multiple_of(8 * offs[c] + g * r, 16), r), :],
            f_sem.at[c],
        )
        cp.start()
        local.append(cp)
    w_cp = pltpu.make_async_copy(weight, wbuf, w_sem)
    w_cp.start()

    def own_rows(c):
        r = CHUNKS[c]
        return (core * 4 + x) * rows_g + offs[c] + zh * (r // 2)

    t_cps = []
    for c in range(n_chunks):
        r = CHUNKS[c]
        cp = pltpu.make_async_copy(
            target.at[pl.ds(pl.multiple_of(own_rows(c), 16), r // 2), :],
            tgt.at[pl.ds(offs[c] // 2, r // 2), :],
            t_sem.at[c],
        )
        cp.start()
        t_cps.append(cp)

    pl.semaphore_wait(barrier, len(grp_peers) + len(all_tp))

    def seg(c, who, lo, n):
        r = CHUNKS[c]
        return fbuf.at[pl.ds(pl.multiple_of(8 * offs[c] + who * r, 16), r), pl.ds(lo, n)]

    def ag_put(c, k, who, lo, n, dev):
        remote(seg(c, who, lo, n), seg(c, who, lo, n), ag_s.at[c, k], ag_r.at[c, k], (dev, t))

    def ag_own(c, k, lo, n, dev):
        r = CHUNKS[c]
        remote(
            features.at[pl.ds(offs[c], r), pl.ds(lo, n)], seg(c, g, lo, n),
            ag_s.at[c, k], ag_r.at[c, k], (dev, t),
        )

    def ag_got(c, k, who, lo, n):
        arrived(seg(c, who, lo, n), ag_s.at[c, k], ag_r.at[c, k])

    b_cols = depth - a_cols

    def start(c):
        ag_own(c, 0, 0, a_cols, zp)
        ag_own(c, 1, 0, depth, yp)
        ag_own(c, 2, 0, depth, ym)
        ag_own(c, 3, a_cols, b_cols, zp)

    def round1(c):
        ag_got(c, 0, zp, 0, a_cols)
        ag_put(c, 4, zp, 0, a_cols, yp)
        ag_put(c, 5, zp, 0, a_cols, ym)

    def round2(c):
        ag_got(c, 1, ym, 0, depth)
        ag_put(c, 6, ym, 0, half, yp)
        ag_put(c, 10, ym, a_cols, b_cols, zp)
        ag_got(c, 2, yp, 0, depth)
        ag_put(c, 7, yp, half, depth - half, ym)
        ag_put(c, 11, yp, a_cols, b_cols, zp)

    def round3(c):
        ag_got(c, 4, zym, 0, a_cols)
        ag_put(c, 8, zym, 0, a_halves[c], yp)
        ag_got(c, 5, zyp, 0, a_cols)
        ag_put(c, 9, zyp, a_halves[c], a_cols - a_halves[c], ym)

    def round4(c):
        ag_got(c, 6, yo, 0, half)
        ag_got(c, 7, yo, half, depth - half)
        ag_put(c, 12, yo, a_cols, b_cols, zp)

    def finish(c):
        ag_got(c, 3, zp, a_cols, b_cols)
        ag_got(c, 10, zym, a_cols, b_cols)
        ag_got(c, 11, zyp, a_cols, b_cols)
        ag_got(c, 8, zyo, 0, a_halves[c])
        ag_got(c, 9, zyo, a_halves[c], a_cols - a_halves[c])
        ag_got(c, 12, zyo, a_cols, b_cols)
        local[c].wait()

    def matmul(c, which, keep, lo, hi):
        r4 = 4 * CHUNKS[c]
        start_row = pl.multiple_of(8 * offs[c] + which * r4, 16)

        def tile(n, _):
            col = pl.ds(pl.multiple_of(n * TILE, TILE), TILE)
            part = jnp.dot(
                fbuf[pl.ds(start_row, r4), :], wbuf[:, col], preferred_element_type=jnp.float32
            )
            if keep:
                hown[pl.ds(0, r4), col] = part
            else:
                hsend[pl.ds(4 * offs[c], r4), col] = part.astype(jnp.bfloat16)
            return 0

        lax.fori_loop(lo, hi, tile, 0)

    n_cols = cols // TILE

    def matmul_other(c, part):
        if part == 0:
            matmul(c, 1 - core, False, 0, n_cols // 2)
            return
        matmul(c, 1 - core, False, n_cols // 2, n_cols)
        rows = pl.ds(4 * offs[c], 4 * CHUNKS[c])
        remote(hsend.at[rows, :], hrecv.at[rows, :], hp_s.at[c], hp_r.at[c], (g, other))

    def matmul_mine(c, part):
        matmul(c, core, True, part * n_cols // 2, (part + 1) * n_cols // 2)

    def own(c):
        return pl.ds(offs[c] // 2, CHUNKS[c] // 2)

    def spread_x(c):
        r = CHUNKS[c]
        base, n = 4 * offs[c], r // 2
        arrived(hrecv.at[pl.ds(base, 4 * r), :], hp_s.at[c], hp_r.at[c])

        def add(i, _):
            lo = pl.multiple_of(i * 16, 16)
            both = hown[pl.ds(lo, 16), :] + hrecv[pl.ds(base + lo, 16), :].astype(jnp.float32)
            hown[pl.ds(lo, 16), :] = both
            hsum[pl.ds(base + lo, 16), :] = both.astype(jnp.bfloat16)
            return 0

        lax.fori_loop(0, 4 * r // 16, add, 0)
        for j in range(2):
            for k in range(3):
                z = 1 - zh if j == 0 else zh
                remote(
                    hsum.at[pl.ds(pl.multiple_of(base + (x_of[k] * 2 + z) * n, 16), n), :],
                    xrecv.at[j, k, own(c), :],
                    rx_s.at[c, j * 3 + k], rx_r.at[c, j * 3 + k], (g, x_peers[k]),
                )

    def sum_x(c, j):
        n = CHUNKS[c] // 2
        z = 1 - zh if j == 0 else zh
        for k in range(3):
            arrived(xrecv.at[j, k, own(c), :], rx_s.at[c, j * 3 + k], rx_r.at[c, j * 3 + k])
        h = hown[pl.ds(pl.multiple_of((x * 2 + z) * n, 16), n), :]
        for k in range(3):
            h = h + xrecv[j, k, own(c), :].astype(jnp.float32)
        return h

    def spread_z(c):
        zsend[own(c), :] = sum_x(c, 0).astype(jnp.bfloat16)
        remote(zsend.at[own(c), :], zrecv.at[own(c), :], rz_s.at[c], rz_r.at[c], (g, z_peer))

    def keep_own(c):
        hid[own(c), :] = sum_x(c, 1)

    def stats(c):
        n = CHUNKS[c] // 2
        rows = own(c)
        arrived(zrecv.at[rows, :], rz_s.at[c], rz_r.at[c])
        h = hid[rows, :] + zrecv[rows, :].astype(jnp.float32)
        hid[rows, :] = h
        t_cps[c].wait()
        gh = gain_ref[...] * h
        s1 = jnp.sum(h * h, axis=1, keepdims=True)
        s2 = jnp.sum(gh * gh, axis=1, keepdims=True)
        s3 = jnp.sum(gh * tgt[rows, :].astype(jnp.float32), axis=1, keepdims=True)
        lane = lax.broadcasted_iota(jnp.int32, (n, 128), 1)
        st_own[rows, :] = jnp.where(lane == 0, s1, jnp.where(lane == 1, s2, s3))
        for k in range(7):
            remote(
                st_own.at[rows, :], st_recv.at[k, rows, :], st_s.at[c, k], st_r.at[c, k], (grp_peers[k], t)
            )

    def grad_rows(c, who_core, who_x, who_z):
        n = CHUNKS[c] // 2
        lo = 8 * offs[c] + who_core * 4 * CHUNKS[c] + (who_x * 2 + who_z) * n
        return gbuf.at[pl.ds(pl.multiple_of(lo, 16), n), :]

    def gradient(c):
        n = CHUNKS[c] // 2
        rows = own(c)
        total = st_own[rows, :]
        for k in range(7):
            arrived(st_recv.at[k, rows, :], st_s.at[c, k], st_r.at[c, k])
            total = total + st_recv[k, rows, :]
        s1, s2, s3 = total[:, 0:1], total[:, 1:2], total[:, 2:3]
        inv = lax.rsqrt(s1 / dout + EPS)
        accepted = jnp.sum(counts_v[...].astype(jnp.float32), keepdims=True)
        first = own_rows(c) // SPEC
        sub = lax.broadcasted_iota(jnp.int32, (SPEC, 128), 0)
        live = jnp.concatenate(
            [(sub < counts_s[first + i]).astype(jnp.float32) for i in range(n // SPEC)], axis=0
        )[:, 0:1]
        scale = live / accepted
        gain = gain_ref[...]
        h = hid[rows, :]
        dev = h * inv * gain - tgt[rows, :].astype(jnp.float32)
        res = scale * dev
        coupling = scale * (inv * s2 - s3)
        grad = inv * gain * res - h * (inv * inv * inv * coupling / dout)
        mine = pl.ds(pl.multiple_of(8 * offs[c] + core * 4 * CHUNKS[c] + place * n, 16), n)
        gbuf[mine, :] = grad.astype(jnp.bfloat16)
        ref = gbuf.at[mine, :]
        remote(ref, ref, gz_s.at[c], gz_r.at[c], (g, z_peer))
        for k in range(3):
            remote(ref, ref, gx_s.at[c, k], gx_r.at[c, k], (g, x_peers[k]))
        remote(ref, ref, gp_s.at[c, 0], gp_r.at[c, 0], (g, other))
        lost = res * dev
        part = loss_acc[...]
        for i in range(n // 8):
            for j in range(cols // 128):
                part = part + lost[8 * i : 8 * i + 8, 128 * j : 128 * j + 128]
        loss_acc[...] = part

    def pass_x(c):
        ref = grad_rows(c, core, x, 1 - zh)
        arrived(ref, gz_s.at[c], gz_r.at[c])
        for k in range(3):
            remote(ref, ref, gx_s.at[c, 3 + k], gx_r.at[c, 3 + k], (g, x_peers[k]))
        remote(ref, ref, gp_s.at[c, 1], gp_r.at[c, 1], (g, other))

    def pass_pair(c):
        for j in range(2):
            for k in range(3):
                ref = grad_rows(c, core, x_from[k], zh if j == 0 else 1 - zh)
                arrived(ref, gx_s.at[c, j * 3 + k], gx_r.at[c, j * 3 + k])
                remote(ref, ref, gp_s.at[c, 2 + j * 3 + k], gp_r.at[c, 2 + j * 3 + k], (g, other))

    def other_grads(c):
        arrived(grad_rows(c, 1 - core, x, zh), gp_s.at[c, 0], gp_r.at[c, 0])
        arrived(grad_rows(c, 1 - core, x, 1 - zh), gp_s.at[c, 1], gp_r.at[c, 1])
        for j in range(2):
            for k in range(3):
                m = 2 + j * 3 + k
                arrived(grad_rows(c, 1 - core, x_from[k], zh if j == 0 else 1 - zh), gp_s.at[c, m], gp_r.at[c, m])

    n_tiles = depth // TILE
    last = n_chunks - 1

    def outer(c, lo, hi):
        rows = pl.ds(8 * offs[c], 8 * CHUNKS[c])

        def tile(i, _):
            k = pl.ds(pl.multiple_of(i * TILE, TILE), TILE)
            for n in range(cols // TILE):
                col = pl.ds(n * TILE, TILE)
                part = lax.dot_general(
                    fbuf[rows, k], gbuf[rows, col], (((0,), (0,)), ((), ())),
                    preferred_element_type=jnp.float32,
                )
                if c > 0:
                    part = part + acc[k, col]
                if c == last:
                    stage[k, col] = part.astype(jnp.bfloat16)
                else:
                    acc[k, col] = part
            if c == last:
                pltpu.make_async_copy(stage.at[k, :], out.at[k, :], o_sem.at[i]).start()
            return 0

        lax.fori_loop(lo, hi, tile, 0)

    loss_acc[...] = jnp.zeros_like(loss_acc)
    mid = n_tiles // 2

    def do(op, c, *args):
        if 0 <= c < n_chunks:
            op(c, *args)

    def outer_first(c):
        other_grads(c)
        outer(c, 0, mid)

    def outer_second(c):
        outer(c, mid, n_tiles)

    start(0)
    round1(0)
    round2(0)
    do(start, 1)
    round3(0)
    do(round1, 1)
    round4(0)
    w_cp.wait()
    for c in range(n_chunks):
        finish(c)
        matmul_other(c, 0)
        do(stats, c - 1)
        do(round2, c + 1)
        do(start, c + 2)
        matmul_other(c, 1)
        do(pass_pair, c - 2)
        matmul_mine(c, 0)
        do(round3, c + 1)
        matmul_mine(c, 1)
        spread_x(c)
        do(gradient, c - 1)
        do(round1, c + 2)
        do(outer_first, c - 2)
        do(round4, c + 1)
        spread_z(c)
        do(pass_x, c - 1)
        keep_own(c)
        do(outer_second, c - 2)
    stats(last)
    do(pass_pair, last - 1)
    gradient(last)
    for k, p in enumerate(all_tp):
        remote(loss_acc, l1_recv.at[k], l1_s.at[k], l1_r.at[k], (g, p))
    do(outer_first, last - 1)
    pass_x(last)
    do(outer_second, last - 1)
    pass_pair(last)
    sum1 = loss_acc[...]
    for k in range(15):
        arrived(l1_recv.at[k], l1_s.at[k], l1_r.at[k])
        sum1 = sum1 + l1_recv[k]
    l2_own[...] = sum1
    for k in range(7):
        remote(l2_own, l2_recv.at[k], l2_s.at[k], l2_r.at[k], (grp_peers[k], t))
    outer_first(last)
    outer_second(last)
    sum2 = l2_own[...]
    for k in range(7):
        arrived(l2_recv.at[k], l2_s.at[k], l2_r.at[k])
        sum2 = sum2 + l2_recv[k]
    loss_out[0, 0] = 0.5 * jnp.sum(sum2)
    for i in range(n_tiles):
        k = pl.ds(i * TILE, TILE)
        pltpu.make_async_copy(stage.at[k, :], out.at[k, :], o_sem.at[i]).wait()
    for cp in sends:
        cp.wait_send()


def shards(features, weight, norm_gain, target, counts):
    rows_g, depth = features.shape
    cols = weight.shape[1]
    total = target.shape[0]
    n = len(CHUNKS)
    bf, f32 = jnp.bfloat16, jnp.float32
    own = total // 16
    dma = pltpu.SemaphoreType.DMA
    anyspace = pl.BlockSpec(memory_space=pl.ANY)
    vmem = pl.BlockSpec(memory_space=pltpu.VMEM)
    unit = depth // 128
    a_units = unit * 15 // 24
    split = (a_units * 128, (a_units // 2) * 128, (unit // 2) * 128)
    out, loss = pl.pallas_call(
        functools.partial(kernel, cols * lax.axis_size("grp"), split),
        out_shape=(
            jax.ShapeDtypeStruct((depth, cols), bf),
            jax.ShapeDtypeStruct((1, 1), f32),
        ),
        in_specs=[anyspace, anyspace, vmem, anyspace, pl.BlockSpec(memory_space=pltpu.SMEM), vmem],
        out_specs=(anyspace, pl.BlockSpec(memory_space=pltpu.SMEM)),
        scratch_shapes=[
            pltpu.VMEM((total, depth), bf),
            pltpu.VMEM((depth, cols), bf),
            pltpu.VMEM((depth, cols), f32),
            pltpu.VMEM((total, cols), bf),
            pltpu.VMEM((depth, cols), bf),
            pltpu.VMEM((total // 2, cols), bf),
            pltpu.VMEM((total // 2, cols), bf),
            pltpu.VMEM((4 * max(CHUNKS), cols), f32),
            pltpu.VMEM((total // 2, cols), bf),
            pltpu.VMEM((2, 3, own, cols), bf),
            pltpu.VMEM((own, cols), bf),
            pltpu.VMEM((own, cols), bf),
            pltpu.VMEM((own, cols), f32),
            pltpu.VMEM((own, cols), bf),
            pltpu.VMEM((own, 128), f32),
            pltpu.VMEM((7, own, 128), f32),
            pltpu.VMEM((8, 128), f32),
            pltpu.VMEM((15, 8, 128), f32),
            pltpu.VMEM((8, 128), f32),
            pltpu.VMEM((7, 8, 128), f32),
            dma, dma((n,)), dma((n,)), dma((depth // TILE,)),
            dma((n, 13)), dma((n, 13)), dma((n,)), dma((n,)), dma((n, 6)), dma((n, 6)), dma((n,)), dma((n,)),
            dma((n, 7)), dma((n, 7)), dma((n,)), dma((n,)), dma((n, 6)), dma((n, 6)), dma((n, 8)), dma((n, 8)),
            dma((15,)), dma((15,)), dma((7,)), dma((7,)),
        ],
        compiler_params=pltpu.CompilerParams(
            collective_id=0, has_side_effects=True, vmem_limit_bytes=64 * 1024 * 1024 - 65536
        ),
    )(features, weight, norm_gain.reshape(1, cols), target, counts, counts.reshape(2, -1))
    return out, loss[0, 0]


def solution(mesh):
    placed = (P("grp", "tp"), P("tp", "grp"), P("grp"), P(None, "grp"), P())
    return jax.shard_map(
        shards, mesh=mesh, in_specs=placed, out_specs=(P("tp", "grp"), P()), check_vma=False
    )
```

```python
import functools

import jax
import jax.numpy as jnp
from jax import lax
from jax.experimental import pallas as pl
from jax.experimental.pallas import tpu as pltpu
from jax.sharding import PartitionSpec as P

SPEC = 8
EPS = 1e-06
CHUNKS = (64, 64, 64, 32, 32)
ORDER = (
    ("start", 0, 0), ("r1", 0, 0), ("r2", 0, 0), ("start", 1, 0), ("r3", 0, 0), ("r4", 0, 0), ("r1", 1, 0),
    ("r2", 1, 0), ("start", 2, 0), ("fin", 0, 0), ("m1", 0, 0), ("m1", 0, 1), ("r3", 1, 0), ("p", 0, 0),
    ("r4", 1, 0), ("r1", 2, 0), ("q1", 0, 0), ("q2", 0, 0), ("r2", 2, 0), ("start", 3, 0), ("s", 0, 0),
    ("fin", 1, 0), ("m1", 1, 0), ("m1", 1, 1), ("r3", 2, 0), ("p", 1, 0), ("r1", 3, 0), ("r4", 2, 0),
    ("q1", 1, 0), ("r2", 3, 0), ("start", 4, 0), ("q2", 1, 0), ("g", 0, 0), ("fin", 2, 0), ("s", 1, 0),
    ("m1", 2, 0), ("r3", 3, 0), ("m1", 2, 1), ("r4", 3, 0), ("r1", 4, 0), ("x", 0, 0), ("p", 2, 0),
    ("h", 0, 0), ("r2", 4, 0), ("fin", 3, 0), ("g", 1, 0), ("m1", 3, 0), ("r3", 4, 0), ("q1", 2, 0),
    ("m1", 3, 1), ("r4", 4, 0), ("h", 1, 0), ("p", 3, 0), ("q2", 2, 0), ("s", 2, 0), ("fin", 4, 0),
    ("m1", 4, 0), ("x", 0, 1), ("m1", 4, 1), ("g", 2, 0), ("x", 1, 0), ("p", 4, 0), ("d", 0, 0), ("x", 1, 1),
    ("d", 0, 1), ("h", 2, 0), ("q1", 3, 0), ("q2", 3, 0), ("d", 1, 0), ("x", 2, 0), ("s", 3, 0), ("d", 1, 1),
    ("q1", 4, 0), ("q2", 4, 0), ("g", 3, 0), ("x", 2, 1), ("s", 4, 0), ("d", 2, 0), ("h", 3, 0), ("x", 3, 0),
    ("g", 4, 0), ("d", 2, 1), ("x", 3, 1), ("h", 4, 0), ("d", 3, 0), ("x", 4, 0), ("d", 3, 1), ("x", 4, 1),
    ("d", 4, 0), ("d", 4, 1),
)
TILE = 256
MESH = pl.DeviceIdType.MESH

TP_OFF = ((0, 1), (0, 3), (0, 2), (1, 0), (1, 1), (1, 3), (1, 2))
X_OFF = (1, 3, 2)
GRP_OFF = ((0, 1), (1, 0), (3, 0), (2, 0), (1, 1), (3, 1), (2, 1))


def kernel(
    dout, split, features, weight, gain_ref, target, counts_s, counts_v, out, loss_out,
    fbuf, wbuf, acc, gbuf, hsend, hrecv, hfull, hsum, xrecv, zsend, zrecv, hid, tgt,
    st_own, st_recv, loss_acc, l1_recv, l2_own, l2_recv,
    w_sem, f_sem, t_sem,
    ag_s, ag_r, hp_s, hp_r, rx_s, rx_r, rz_s, rz_r, st_s, st_r, gz_s, gz_r, gx_s, gx_r, gp_s, gp_r,
    l1_s, l1_r, l2_s, l2_r,
):
    g, t = lax.axis_index("grp"), lax.axis_index("tp")
    y, zl = g // 2, lax.rem(g, 2)
    core, q = lax.rem(t, 2), t // 2
    zh, x = q // 4, lax.rem(q, 4)
    depth, cols = wbuf.shape
    rows_g = features.shape[0]
    n_chunks = len(CHUNKS)
    offs = [sum(CHUNKS[:c]) for c in range(n_chunks)]
    a_cols, a_low, half = split
    a_halves = [a_low if c % 2 == 0 else a_cols - a_low for c in range(n_chunks)]
    place = x * 2 + zh

    def grp_dev(dy, dz):
        return lax.rem(y + dy, 4) * 2 + lax.rem(zl + dz, 2)

    def chip(dz, dx):
        return lax.rem(zh + dz, 2) * 4 + lax.rem(x + dx, 4)

    zp, yp, ym, yo = grp_dev(0, 1), grp_dev(1, 0), grp_dev(3, 0), grp_dev(2, 0)
    zyp, zym, zyo = grp_dev(1, 1), grp_dev(3, 1), grp_dev(2, 1)
    other = t + 1 - 2 * core

    tp_peers = [chip(*o) * 2 + core for o in TP_OFF]
    x_peers, z_peer = tp_peers[:3], tp_peers[3]
    x_of = [lax.rem(x + dx, 4) for dx in X_OFF]
    x_from = [lax.rem(x + 4 - dx, 4) for dx in X_OFF]
    grp_peers = [grp_dev(*o) for o in GRP_OFF]
    all_tp = tp_peers + [chip(*o) * 2 + 1 - core for o in TP_OFF] + [other]

    barrier = pltpu.get_barrier_semaphore()
    for p in grp_peers:
        pl.semaphore_signal(barrier, inc=1, device_id=(p, t), device_id_type=MESH)
    for p in all_tp:
        pl.semaphore_signal(barrier, inc=1, device_id=(g, p), device_id_type=MESH)

    sends = []

    def remote(src, dst, ssem, rsem, dev):
        cp = pltpu.make_async_remote_copy(
            src_ref=src, dst_ref=dst, send_sem=ssem, recv_sem=rsem, device_id=dev, device_id_type=MESH
        )
        cp.start()
        sends.append(cp)

    def arrived(dst, ssem, rsem):
        pltpu.make_async_remote_copy(
            src_ref=dst, dst_ref=dst, send_sem=ssem, recv_sem=rsem, device_id=(zp, t), device_id_type=MESH
        ).wait_recv()

    local = []
    for c in range(n_chunks):
        r = CHUNKS[c]
        cp = pltpu.make_async_copy(
            features.at[pl.ds(offs[c], r), :],
            fbuf.at[pl.ds(pl.multiple_of(8 * offs[c] + g * r, 16), r), :],
            f_sem.at[c],
        )
        cp.start()
        local.append(cp)
    w_cp = pltpu.make_async_copy(weight, wbuf, w_sem)
    w_cp.start()

    def own_rows(c):
        r = CHUNKS[c]
        return (core * 4 + x) * rows_g + offs[c] + zh * (r // 2)

    t_cps = []
    for c in range(n_chunks):
        r = CHUNKS[c]
        cp = pltpu.make_async_copy(
            target.at[pl.ds(pl.multiple_of(own_rows(c), 16), r // 2), :],
            tgt.at[pl.ds(offs[c] // 2, r // 2), :],
            t_sem.at[c],
        )
        cp.start()
        t_cps.append(cp)

    pl.semaphore_wait(barrier, len(grp_peers) + len(all_tp))

    def seg(c, who, lo, n):
        r = CHUNKS[c]
        return fbuf.at[pl.ds(pl.multiple_of(8 * offs[c] + who * r, 16), r), pl.ds(lo, n)]

    def ag_put(c, k, who, lo, n, dev):
        remote(seg(c, who, lo, n), seg(c, who, lo, n), ag_s.at[c, k], ag_r.at[c, k], (dev, t))

    def ag_own(c, k, lo, n, dev):
        r = CHUNKS[c]
        remote(
            features.at[pl.ds(offs[c], r), pl.ds(lo, n)], seg(c, g, lo, n),
            ag_s.at[c, k], ag_r.at[c, k], (dev, t),
        )

    def ag_got(c, k, who, lo, n):
        arrived(seg(c, who, lo, n), ag_s.at[c, k], ag_r.at[c, k])

    b_cols = depth - a_cols

    def start(c):
        ag_own(c, 0, 0, a_cols, zp)
        ag_own(c, 1, 0, depth, yp)
        ag_own(c, 2, 0, depth, ym)
        ag_own(c, 3, a_cols, b_cols, zp)

    def round1(c):
        ag_got(c, 0, zp, 0, a_cols)
        ag_put(c, 4, zp, 0, a_cols, yp)
        ag_put(c, 5, zp, 0, a_cols, ym)

    def round2(c):
        ag_got(c, 1, ym, 0, depth)
        ag_put(c, 6, ym, 0, half, yp)
        ag_put(c, 10, ym, a_cols, b_cols, zp)
        ag_got(c, 2, yp, 0, depth)
        ag_put(c, 7, yp, half, depth - half, ym)
        ag_put(c, 11, yp, a_cols, b_cols, zp)

    def round3(c):
        ag_got(c, 4, zym, 0, a_cols)
        ag_put(c, 8, zym, 0, a_halves[c], yp)
        ag_got(c, 5, zyp, 0, a_cols)
        ag_put(c, 9, zyp, a_halves[c], a_cols - a_halves[c], ym)

    def round4(c):
        ag_got(c, 6, yo, 0, half)
        ag_got(c, 7, yo, half, depth - half)
        ag_put(c, 12, yo, a_cols, b_cols, zp)

    def finish(c):
        ag_got(c, 3, zp, a_cols, b_cols)
        ag_got(c, 10, zym, a_cols, b_cols)
        ag_got(c, 11, zyp, a_cols, b_cols)
        ag_got(c, 8, zyo, 0, a_halves[c])
        ag_got(c, 9, zyo, a_halves[c], a_cols - a_halves[c])
        ag_got(c, 12, zyo, a_cols, b_cols)
        local[c].wait()

    n_cols = cols // TILE
    parts = 2

    def matmul(c, part):
        r8 = 8 * CHUNKS[c]
        rows = pl.ds(8 * offs[c], r8)

        def tile(n, _):
            col = pl.ds(pl.multiple_of(n * TILE, TILE), TILE)
            prod = jnp.dot(fbuf[rows, :], wbuf[:, col], preferred_element_type=jnp.float32)
            hfull[c % 2, pl.ds(0, r8), col] = prod
            hsend[rows, col] = prod.astype(jnp.bfloat16)
            return 0

        lax.fori_loop(part * n_cols // parts, (part + 1) * n_cols // parts, tile, 0)
        wide = pl.ds(part * cols // parts, cols // parts)
        theirs = pl.ds(pl.multiple_of(8 * offs[c] + (1 - core) * (r8 // 2), 16), r8 // 2)
        remote(
            hsend.at[theirs, wide], hrecv.at[pl.ds(4 * offs[c], r8 // 2), wide],
            hp_s.at[c, part], hp_r.at[c, part], (g, other),
        )

    def mine(c, lo, n):
        return c % 2, pl.ds(pl.multiple_of(core * 4 * CHUNKS[c] + lo, 16), n)

    def own(c):
        return pl.ds(offs[c] // 2, CHUNKS[c] // 2)

    def spread_x(c):
        r = CHUNKS[c]
        base, n = 4 * offs[c], r // 2
        for i in range(parts):
            wide = pl.ds(i * cols // parts, cols // parts)
            arrived(hrecv.at[pl.ds(base, 4 * r), wide], hp_s.at[c, i], hp_r.at[c, i])

        def add(i, _):
            lo = pl.multiple_of(i * 16, 16)
            slot, rows = mine(c, lo, 16)
            both = hfull[slot, rows, :] + hrecv[pl.ds(base + lo, 16), :].astype(jnp.float32)
            hfull[slot, rows, :] = both
            hsum[pl.ds(base + lo, 16), :] = both.astype(jnp.bfloat16)
            return 0

        lax.fori_loop(0, 4 * r // 16, add, 0)
        for j in range(2):
            for k in range(3):
                z = 1 - zh if j == 0 else zh
                remote(
                    hsum.at[pl.ds(pl.multiple_of(base + (x_of[k] * 2 + z) * n, 16), n), :],
                    xrecv.at[j, k, own(c), :],
                    rx_s.at[c, j * 3 + k], rx_r.at[c, j * 3 + k], (g, x_peers[k]),
                )

    def sum_x(c, j):
        n = CHUNKS[c] // 2
        z = 1 - zh if j == 0 else zh
        for k in range(3):
            arrived(xrecv.at[j, k, own(c), :], rx_s.at[c, j * 3 + k], rx_r.at[c, j * 3 + k])
        slot, rows = mine(c, (x * 2 + z) * n, n)
        h = hfull[slot, rows, :]
        for k in range(3):
            h = h + xrecv[j, k, own(c), :].astype(jnp.float32)
        return h

    def spread_z(c):
        zsend[own(c), :] = sum_x(c, 0).astype(jnp.bfloat16)
        remote(zsend.at[own(c), :], zrecv.at[own(c), :], rz_s.at[c], rz_r.at[c], (g, z_peer))

    def keep_own(c):
        hid[own(c), :] = sum_x(c, 1)

    def stats(c):
        n = CHUNKS[c] // 2
        rows = own(c)
        arrived(zrecv.at[rows, :], rz_s.at[c], rz_r.at[c])
        h = hid[rows, :] + zrecv[rows, :].astype(jnp.float32)
        hid[rows, :] = h
        t_cps[c].wait()
        gh = gain_ref[...] * h
        s1 = jnp.sum(h * h, axis=1, keepdims=True)
        s2 = jnp.sum(gh * gh, axis=1, keepdims=True)
        s3 = jnp.sum(gh * tgt[rows, :].astype(jnp.float32), axis=1, keepdims=True)
        lane = lax.broadcasted_iota(jnp.int32, (n, 128), 1)
        wide = jnp.where(lane == 0, s1, jnp.where(lane == 1, s2, s3))
        wide = jnp.concatenate([wide, jnp.zeros((128 - n, 128), jnp.float32)], axis=0)
        st_own[c] = jnp.transpose(wide)[0:8, :]
        for k in range(7):
            remote(st_own.at[c], st_recv.at[c, k], st_s.at[c, k], st_r.at[c, k], (grp_peers[k], t))

    def grad_rows(c, who_core, who_x, who_z):
        n = CHUNKS[c] // 2
        lo = 8 * offs[c] + who_core * 4 * CHUNKS[c] + (who_x * 2 + who_z) * n
        return gbuf.at[pl.ds(pl.multiple_of(lo, 16), n), :]

    def gradient(c):
        n = CHUNKS[c] // 2
        rows = own(c)
        total = st_own[c]
        for k in range(7):
            arrived(st_recv.at[c, k], st_s.at[c, k], st_r.at[c, k])
            total = total + st_recv[c, k]
        total = jnp.concatenate([total, jnp.zeros((120, 128), jnp.float32)], axis=0)
        total = jnp.transpose(total)[0:n, :]
        s1, s2, s3 = total[:, 0:1], total[:, 1:2], total[:, 2:3]
        inv = lax.rsqrt(s1 / dout + EPS)
        accepted = jnp.sum(counts_v[...].astype(jnp.float32), keepdims=True)
        first = own_rows(c) // SPEC
        sub = lax.broadcasted_iota(jnp.int32, (SPEC, 128), 0)
        live = jnp.concatenate(
            [(sub < counts_s[first + i]).astype(jnp.float32) for i in range(n // SPEC)], axis=0
        )[:, 0:1]
        scale = live / accepted
        gain = gain_ref[...]
        h = hid[rows, :]
        dev = h * inv * gain - tgt[rows, :].astype(jnp.float32)
        res = scale * dev
        coupling = scale * (inv * s2 - s3)
        grad = inv * gain * res - h * (inv * inv * inv * coupling / dout)
        mine = pl.ds(pl.multiple_of(8 * offs[c] + core * 4 * CHUNKS[c] + place * n, 16), n)
        gbuf[mine, :] = grad.astype(jnp.bfloat16)
        ref = gbuf.at[mine, :]
        remote(ref, ref, gz_s.at[c], gz_r.at[c], (g, z_peer))
        for k in range(3):
            remote(ref, ref, gx_s.at[c, k], gx_r.at[c, k], (g, x_peers[k]))
        remote(ref, ref, gp_s.at[c, 0], gp_r.at[c, 0], (g, other))
        lost = res * dev
        part = loss_acc[...]
        for i in range(n // 8):
            for j in range(cols // 128):
                part = part + lost[8 * i : 8 * i + 8, 128 * j : 128 * j + 128]
        loss_acc[...] = part

    def pass_x(c):
        ref = grad_rows(c, core, x, 1 - zh)
        arrived(ref, gz_s.at[c], gz_r.at[c])
        for k in range(3):
            remote(ref, ref, gx_s.at[c, 3 + k], gx_r.at[c, 3 + k], (g, x_peers[k]))
        remote(ref, ref, gp_s.at[c, 1], gp_r.at[c, 1], (g, other))

    def pass_pair(c, j):
        for k in range(3):
            ref = grad_rows(c, core, x_from[k], zh if j == 0 else 1 - zh)
            arrived(ref, gx_s.at[c, j * 3 + k], gx_r.at[c, j * 3 + k])
            remote(ref, ref, gp_s.at[c, 2 + j * 3 + k], gp_r.at[c, 2 + j * 3 + k], (g, other))

    def other_grads(c):
        arrived(grad_rows(c, 1 - core, x, zh), gp_s.at[c, 0], gp_r.at[c, 0])
        arrived(grad_rows(c, 1 - core, x, 1 - zh), gp_s.at[c, 1], gp_r.at[c, 1])
        for j in range(2):
            for k in range(3):
                m = 2 + j * 3 + k
                arrived(grad_rows(c, 1 - core, x_from[k], zh if j == 0 else 1 - zh), gp_s.at[c, m], gp_r.at[c, m])

    n_tiles = depth // TILE
    last = n_chunks - 1

    def outer(c, part):
        if part == 0:
            other_grads(c)
        rows = pl.ds(8 * offs[c], 8 * CHUNKS[c])

        def tile(i, _):
            k = pl.ds(pl.multiple_of(i * TILE, TILE), TILE)
            for n in range(n_cols):
                col = pl.ds(n * TILE, TILE)
                prod = lax.dot_general(
                    fbuf[rows, k], gbuf[rows, col], (((0,), (0,)), ((), ())),
                    preferred_element_type=jnp.float32,
                )
                if c > 0:
                    prod = prod + acc[k, col]
                if c == last:
                    out[k, col] = prod.astype(jnp.bfloat16)
                else:
                    acc[k, col] = prod
            return 0

        lax.fori_loop(part * n_tiles // 2, (part + 1) * n_tiles // 2, tile, 0)

    def share_loss():
        for k, p in enumerate(all_tp):
            remote(loss_acc, l1_recv.at[k], l1_s.at[k], l1_r.at[k], (g, p))

    def pass_loss():
        total = loss_acc[...]
        for k in range(15):
            arrived(l1_recv.at[k], l1_s.at[k], l1_r.at[k])
            total = total + l1_recv[k]
        l2_own[...] = total
        for k in range(7):
            remote(l2_own, l2_recv.at[k], l2_s.at[k], l2_r.at[k], (grp_peers[k], t))

    loss_acc[...] = jnp.zeros_like(loss_acc)
    steps = {
        "start": start, "r1": round1, "r2": round2, "r3": round3, "r4": round4, "fin": finish,
        "p": spread_x, "q1": spread_z, "q2": keep_own, "s": stats, "g": gradient, "h": pass_x,
    }
    parted = {"m1": matmul, "x": pass_pair, "d": outer}
    for step, c, part in ORDER:
        if (step, c, part) == ("m1", 0, 0):
            w_cp.wait()
        if (step, c, part) == ("d", last, 0):
            pass_loss()
        if step in parted:
            parted[step](c, part)
        else:
            steps[step](c)
        if (step, c) == ("g", last):
            share_loss()
    sum2 = l2_own[...]
    for k in range(7):
        arrived(l2_recv.at[k], l2_s.at[k], l2_r.at[k])
        sum2 = sum2 + l2_recv[k]
    loss_out[0, 0] = 0.5 * jnp.sum(sum2)
    for cp in sends:
        cp.wait_send()


def shards(features, weight, norm_gain, target, counts):
    rows_g, depth = features.shape
    cols = weight.shape[1]
    total = target.shape[0]
    n = len(CHUNKS)
    bf, f32 = jnp.bfloat16, jnp.float32
    own = total // 16
    dma = pltpu.SemaphoreType.DMA
    anyspace = pl.BlockSpec(memory_space=pl.ANY)
    vmem = pl.BlockSpec(memory_space=pltpu.VMEM)
    unit = depth // 128
    a_units = unit * 15 // 24
    split = (a_units * 128, (a_units // 2) * 128, (unit // 2) * 128)
    out, loss = pl.pallas_call(
        functools.partial(kernel, cols * lax.axis_size("grp"), split),
        out_shape=(
            pltpu.VMEM((depth, cols), bf),
            jax.ShapeDtypeStruct((1, 1), f32),
        ),
        in_specs=[anyspace, anyspace, vmem, anyspace, pl.BlockSpec(memory_space=pltpu.SMEM), vmem],
        out_specs=(vmem, pl.BlockSpec(memory_space=pltpu.SMEM)),
        scratch_shapes=[
            pltpu.VMEM((total, depth), bf),
            pltpu.VMEM((depth, cols), bf),
            pltpu.VMEM((depth, cols), f32),
            pltpu.VMEM((total, cols), bf),
            pltpu.VMEM((total, cols), bf),
            pltpu.VMEM((total // 2, cols), bf),
            pltpu.VMEM((2, 8 * max(CHUNKS), cols), f32),
            pltpu.VMEM((total // 2, cols), bf),
            pltpu.VMEM((2, 3, own, cols), bf),
            pltpu.VMEM((own, cols), bf),
            pltpu.VMEM((own, cols), bf),
            pltpu.VMEM((own, cols), f32),
            pltpu.VMEM((own, cols), bf),
            pltpu.VMEM((n, 8, 128), f32),
            pltpu.VMEM((n, 7, 8, 128), f32),
            pltpu.VMEM((8, 128), f32),
            pltpu.VMEM((15, 8, 128), f32),
            pltpu.VMEM((8, 128), f32),
            pltpu.VMEM((7, 8, 128), f32),
            dma, dma((n,)), dma((n,)),
            dma((n, 13)), dma((n, 13)), dma((n, 2)), dma((n, 2)), dma((n, 6)), dma((n, 6)), dma((n,)), dma((n,)),
            dma((n, 7)), dma((n, 7)), dma((n,)), dma((n,)), dma((n, 6)), dma((n, 6)), dma((n, 8)), dma((n, 8)),
            dma((15,)), dma((15,)), dma((7,)), dma((7,)),
        ],
        compiler_params=pltpu.CompilerParams(
            collective_id=0, has_side_effects=True, vmem_limit_bytes=54 * 1024 * 1024
        ),
    )(features, weight, norm_gain.reshape(1, cols), target, counts, counts.reshape(2, -1))
    return out, loss[0, 0]


def solution(mesh):
    placed = (P("grp", "tp"), P("tp", "grp"), P("grp"), P(None, "grp"), P())
    return jax.shard_map(
        shards, mesh=mesh, in_specs=placed, out_specs=(P("tp", "grp"), P()), check_vma=False
    )
```

```python
import functools

import jax
import jax.numpy as jnp
from jax import lax
from jax.experimental import pallas as pl
from jax.experimental.pallas import tpu as pltpu
from jax.sharding import PartitionSpec as P

SPEC = 8
EPS = 1e-06
CHUNKS = (32, 32, 32, 32, 32, 32, 32, 32)
GROUPS = ((0, 1), (2, 3), (4, 5), (6,), (7,))
ORDER = (
    ("za", 0, 0), ("o1", 0, 0), ("o2", 0, 0), ("zb", 0, 0), ("za", 1, 0), ("o1", 1, 0), ("r2", 0, 0),
    ("r1", 0, 0), ("zb", 1, 0), ("r5", 0, 0), ("r2", 1, 0), ("r1", 1, 0), ("r4", 0, 0), ("za", 2, 0),
    ("r3", 0, 0), ("zb", 2, 0), ("r4", 1, 0), ("o2", 1, 0), ("r3", 1, 0), ("r1", 2, 0), ("za", 3, 0),
    ("fin", 0, 0), ("m1", 0, 0), ("m1", 0, 1), ("r5", 1, 0), ("o1", 2, 0), ("p", 0, 0), ("r1", 3, 0),
    ("zb", 3, 0), ("r3", 2, 0), ("za", 4, 0), ("r2", 2, 0), ("q1", 0, 0), ("fin", 1, 0), ("m1", 1, 0),
    ("r3", 3, 0), ("zb", 4, 0), ("q2", 0, 0), ("m1", 1, 1), ("o2", 2, 0), ("za", 5, 0), ("r1", 4, 0),
    ("p", 1, 0), ("r4", 2, 0), ("s", 0, 0), ("o1", 3, 0), ("zb", 5, 0), ("r5", 2, 0), ("q1", 1, 0),
    ("r1", 5, 0), ("q2", 1, 0), ("r3", 4, 0), ("g", 0, 0), ("r2", 3, 0), ("za", 6, 0), ("r3", 5, 0),
    ("fin", 2, 0), ("x", 0, 0), ("o2", 3, 0), ("zb", 6, 0), ("m1", 2, 0), ("s", 1, 0), ("r4", 3, 0),
    ("h", 0, 0), ("m1", 2, 1), ("r1", 6, 0), ("za", 7, 0), ("p", 2, 0), ("r5", 3, 0), ("o1", 4, 0),
    ("x", 0, 1), ("o2", 4, 0), ("g", 1, 0), ("r3", 6, 0), ("q1", 2, 0), ("r1", 7, 0), ("r2", 4, 0),
    ("q2", 2, 0), ("zb", 7, 0), ("x", 1, 0), ("r5", 4, 0), ("fin", 3, 0), ("m1", 3, 0), ("o1", 5, 0),
    ("h", 1, 0), ("m1", 3, 1), ("r3", 7, 0), ("s", 2, 0), ("p", 3, 0), ("r4", 4, 0), ("o2", 5, 0), ("x", 1, 1),
    ("r2", 5, 0), ("fin", 4, 0), ("q1", 3, 0), ("m1", 4, 0), ("r5", 5, 0), ("o1", 6, 0), ("g", 2, 0),
    ("q2", 3, 0), ("m1", 4, 1), ("r4", 5, 0), ("o2", 6, 0), ("s", 3, 0), ("d", 0, 0), ("o1", 7, 0),
    ("r2", 6, 0), ("x", 2, 0), ("p", 4, 0), ("d", 0, 1), ("r5", 6, 0), ("h", 2, 0), ("d", 0, 2), ("o2", 7, 0),
    ("fin", 5, 0), ("m1", 5, 0), ("r2", 7, 0), ("g", 3, 0), ("q1", 4, 0), ("q2", 4, 0), ("m1", 5, 1),
    ("r4", 6, 0), ("x", 2, 1), ("d", 0, 3), ("r5", 7, 0), ("h", 3, 0), ("x", 3, 0), ("p", 5, 0), ("s", 4, 0),
    ("r4", 7, 0), ("fin", 6, 0), ("m1", 6, 0), ("x", 3, 1), ("m1", 6, 1), ("q1", 5, 0), ("p", 6, 0),
    ("g", 4, 0), ("q2", 5, 0), ("fin", 7, 0), ("m1", 7, 0), ("s", 5, 0), ("m1", 7, 1), ("h", 4, 0),
    ("q1", 6, 0), ("d", 1, 0), ("p", 7, 0), ("x", 4, 0), ("g", 5, 0), ("q2", 6, 0), ("s", 6, 0), ("d", 1, 1),
    ("x", 4, 1), ("d", 1, 2), ("h", 5, 0), ("q1", 7, 0), ("d", 1, 3), ("g", 6, 0), ("q2", 7, 0), ("x", 5, 0),
    ("s", 7, 0), ("x", 5, 1), ("h", 6, 0), ("x", 6, 0), ("g", 7, 0), ("d", 2, 0), ("x", 6, 1), ("d", 2, 1),
    ("h", 7, 0), ("d", 2, 2), ("x", 7, 0), ("d", 2, 3), ("d", 3, 0), ("x", 7, 1), ("d", 3, 1), ("d", 3, 2),
    ("d", 3, 3), ("d", 4, 0), ("d", 4, 1), ("d", 4, 2), ("d", 4, 3),
)
TILE = 256
RING = 64
AG_SEM = (0, 1, 2, 3, 4, 5, 6, 7, 8, 8, 3, 3, 3, 9, 10)
MESH = pl.DeviceIdType.MESH

TP_OFF = ((0, 1), (0, 3), (0, 2), (1, 0), (1, 1), (1, 3), (1, 2))
X_OFF = (1, 3, 2)
GRP_OFF = ((0, 1), (1, 0), (3, 0), (2, 0), (1, 1), (3, 1), (2, 1))


def kernel(
    dout, split, features, weight, gain_ref, target, counts_s, counts_v, out, loss_out,
    fbuf, wbuf, acc, gbuf, hsend, hrecv, hfull, hsum, xrecv, zsend, zrecv, hid, tgt,
    st_own, st_recv, loss_acc, l1_recv, l2_own, l2_recv,
    w_sem, f_sem, t_sem, send_sem,
    ag_r, hp_r, rx_r, rz_r, st_r, gz_r, gx_r, gp_r,
    l1_r, l2_r,
):
    g, t = lax.axis_index("grp"), lax.axis_index("tp")
    y, zl = g // 2, lax.rem(g, 2)
    core, q = lax.rem(t, 2), t // 2
    zh, x = q // 4, lax.rem(q, 4)
    depth, cols = wbuf.shape
    rows_g = features.shape[0]
    n_chunks = len(CHUNKS)
    offs = [sum(CHUNKS[:c]) for c in range(n_chunks)]
    a_cols, a_low, half = split
    a_halves = [a_low if c % 2 == 0 else a_cols - a_low for c in range(n_chunks)]
    place = x * 2 + zh

    def grp_dev(dy, dz):
        return lax.rem(y + dy, 4) * 2 + lax.rem(zl + dz, 2)

    def chip(dz, dx):
        return lax.rem(zh + dz, 2) * 4 + lax.rem(x + dx, 4)

    zp, yp, ym, yo = grp_dev(0, 1), grp_dev(1, 0), grp_dev(3, 0), grp_dev(2, 0)
    zyp, zym, zyo = grp_dev(1, 1), grp_dev(3, 1), grp_dev(2, 1)
    other = t + 1 - 2 * core

    tp_peers = [chip(*o) * 2 + core for o in TP_OFF]
    x_peers, z_peer = tp_peers[:3], tp_peers[3]
    x_of = [lax.rem(x + dx, 4) for dx in X_OFF]
    x_from = [lax.rem(x + 4 - dx, 4) for dx in X_OFF]
    grp_peers = [grp_dev(*o) for o in GRP_OFF]
    all_tp = tp_peers + [chip(*o) * 2 + 1 - core for o in TP_OFF] + [other]

    barrier = pltpu.get_barrier_semaphore()
    for p in grp_peers:
        pl.semaphore_signal(barrier, inc=1, device_id=(p, t), device_id_type=MESH)
    for p in all_tp:
        pl.semaphore_signal(barrier, inc=1, device_id=(g, p), device_id_type=MESH)

    sends = []

    sent = [0]

    def remote(src, dst, rsem, dev):
        if len(sends) == RING:
            sends.pop(0).wait_send()
        cp = pltpu.make_async_remote_copy(
            src_ref=src, dst_ref=dst, send_sem=send_sem.at[sent[0] % RING], recv_sem=rsem,
            device_id=dev, device_id_type=MESH,
        )
        cp.start()
        sends.append(cp)
        sent[0] += 1

    def arrived(dst, rsem):
        pltpu.make_async_remote_copy(
            src_ref=dst, dst_ref=dst, send_sem=send_sem.at[0], recv_sem=rsem,
            device_id=(zp, t), device_id_type=MESH,
        ).wait_recv()

    def slot_of(who):
        return lax.rem(who, 2) * 4 + who // 2

    local = []
    for c in range(n_chunks):
        r = CHUNKS[c]
        cp = pltpu.make_async_copy(
            features.at[pl.ds(offs[c], r), :],
            fbuf.at[pl.ds(pl.multiple_of(8 * offs[c] + slot_of(g) * r, 16), r), :],
            f_sem.at[c],
        )
        cp.start()
        local.append(cp)
    w_cp = pltpu.make_async_copy(weight, wbuf, w_sem)
    w_cp.start()

    def own_rows(c):
        r = CHUNKS[c]
        return (x * 2 + core) * rows_g + offs[c] + zh * (r // 2)

    t_cps = []
    for c in range(n_chunks):
        r = CHUNKS[c]
        cp = pltpu.make_async_copy(
            target.at[pl.ds(pl.multiple_of(own_rows(c), 16), r // 2), :],
            tgt.at[pl.ds(offs[c] // 2, r // 2), :],
            t_sem.at[c],
        )
        cp.start()
        t_cps.append(cp)

    pl.semaphore_wait(barrier, len(grp_peers) + len(all_tp))

    def seg(c, who, lo, n):
        r = CHUNKS[c]
        return fbuf.at[pl.ds(pl.multiple_of(8 * offs[c] + slot_of(who) * r, 16), r), pl.ds(lo, n)]

    def ag_put(c, k, who, lo, n, dev):
        remote(seg(c, who, lo, n), seg(c, who, lo, n), ag_r.at[c, AG_SEM[k]], (dev, t))

    def ag_own(c, k, lo, n, dev):
        r = CHUNKS[c]
        remote(
            features.at[pl.ds(offs[c], r), pl.ds(lo, n)], seg(c, g, lo, n),
            ag_r.at[c, AG_SEM[k]], (dev, t),
        )

    def ag_got(c, k, who, lo, n):
        arrived(seg(c, who, lo, n), ag_r.at[c, AG_SEM[k]])

    b_cols = depth - a_cols

    rest = depth - half

    def own_z_first(c):
        ag_own(c, 0, 0, a_cols, zp)

    def own_z_second(c):
        ag_own(c, 3, a_cols, b_cols, zp)

    def own_y_first(c):
        ag_own(c, 1, 0, half, yp)
        ag_own(c, 2, half, rest, ym)

    def own_y_second(c):
        ag_own(c, 13, half, rest, yp)
        ag_own(c, 14, 0, half, ym)

    def round1(c):
        ag_got(c, 0, zp, 0, a_cols)
        ag_put(c, 4, zp, 0, a_cols, yp)
        ag_put(c, 5, zp, 0, a_cols, ym)

    def round2(c):
        ag_got(c, 1, ym, 0, half)
        ag_put(c, 6, ym, 0, half, yp)
        ag_got(c, 2, yp, half, rest)
        ag_put(c, 7, yp, half, rest, ym)

    def round3(c):
        ag_got(c, 4, zym, 0, a_cols)
        ag_put(c, 8, zym, 0, a_halves[c], yp)
        ag_got(c, 5, zyp, 0, a_cols)
        ag_put(c, 9, zyp, a_halves[c], a_cols - a_halves[c], ym)

    def round4(c):
        ag_got(c, 7, yo, half, rest)
        ag_put(c, 12, yo, a_cols, b_cols, zp)

    def round5(c):
        ag_got(c, 13, ym, half, rest)
        ag_put(c, 10, ym, a_cols, b_cols, zp)
        ag_put(c, 11, yp, a_cols, b_cols, zp)

    def finish(c):
        r = CHUNKS[c]
        ag_got(c, 6, yo, 0, half)
        ag_got(c, 14, yp, 0, half)
        ag_got(c, 8, zyo, 0, a_cols)
        plane = pl.ds(pl.multiple_of(8 * offs[c] + (1 - zl) * 4 * r, 16), 4 * r)
        arrived(fbuf.at[plane, pl.ds(a_cols, b_cols)], ag_r.at[c, AG_SEM[3]])
        local[c].wait()

    n_cols = cols // TILE
    parts = 2

    def matmul(c, part):
        r8 = 8 * CHUNKS[c]
        rows = pl.ds(8 * offs[c], r8)

        def tile(n, _):
            col = pl.ds(pl.multiple_of(n * TILE, TILE), TILE)
            prod = jnp.dot(fbuf[rows, :], wbuf[:, col], preferred_element_type=jnp.float32)
            hfull[c % 2, pl.ds(0, r8), col] = prod
            hsend[rows, col] = prod.astype(jnp.bfloat16)
            return 0

        lax.fori_loop(part * n_cols // parts, (part + 1) * n_cols // parts, tile, 0)
        wide = pl.ds(part * cols // parts, cols // parts)
        theirs = pl.ds(pl.multiple_of(8 * offs[c] + (1 - core) * (r8 // 2), 16), r8 // 2)
        remote(
            hsend.at[theirs, wide], hrecv.at[pl.ds(4 * offs[c], r8 // 2), wide],
            hp_r.at[c, part], (g, other),
        )

    def mine(c, lo, n):
        return c % 2, pl.ds(pl.multiple_of(core * 4 * CHUNKS[c] + lo, 16), n)

    def own(c):
        return pl.ds(offs[c] // 2, CHUNKS[c] // 2)

    def spread_x(c):
        r = CHUNKS[c]
        base, n = 4 * offs[c], r // 2
        for i in range(parts):
            wide = pl.ds(i * cols // parts, cols // parts)
            arrived(hrecv.at[pl.ds(base, 4 * r), wide], hp_r.at[c, i])

        def add(i, _):
            lo = pl.multiple_of(i * 16, 16)
            slot, rows = mine(c, lo, 16)
            both = hfull[slot, rows, :] + hrecv[pl.ds(base + lo, 16), :].astype(jnp.float32)
            hfull[slot, rows, :] = both
            hsum[pl.ds(base + lo, 16), :] = both.astype(jnp.bfloat16)
            return 0

        lax.fori_loop(0, 4 * r // 16, add, 0)
        for j in range(2):
            for k in range(3):
                z = 1 - zh if j == 0 else zh
                remote(
                    hsum.at[pl.ds(pl.multiple_of(base + (x_of[k] * 2 + z) * n, 16), n), :],
                    xrecv.at[j, k, own(c), :],
                    rx_r.at[c, j], (g, x_peers[k]),
                )

    def sum_x(c, j):
        n = CHUNKS[c] // 2
        z = 1 - zh if j == 0 else zh
        arrived(xrecv.at[j, :, own(c), :], rx_r.at[c, j])
        slot, rows = mine(c, (x * 2 + z) * n, n)
        h = hfull[slot, rows, :]
        for k in range(3):
            h = h + xrecv[j, k, own(c), :].astype(jnp.float32)
        return h

    def spread_z(c):
        zsend[own(c), :] = sum_x(c, 0).astype(jnp.bfloat16)
        remote(zsend.at[own(c), :], zrecv.at[own(c), :], rz_r.at[c], (g, z_peer))

    def keep_own(c):
        hid[own(c), :] = sum_x(c, 1)

    def stats(c):
        n = CHUNKS[c] // 2
        rows = own(c)
        arrived(zrecv.at[rows, :], rz_r.at[c])
        h = hid[rows, :] + zrecv[rows, :].astype(jnp.float32)
        hid[rows, :] = h
        t_cps[c].wait()
        gh = gain_ref[...] * h
        s1 = jnp.sum(h * h, axis=1, keepdims=True)
        s2 = jnp.sum(gh * gh, axis=1, keepdims=True)
        s3 = jnp.sum(gh * tgt[rows, :].astype(jnp.float32), axis=1, keepdims=True)
        lane = lax.broadcasted_iota(jnp.int32, (n, 128), 1)
        wide = jnp.where(lane == 0, s1, jnp.where(lane == 1, s2, s3))
        wide = jnp.concatenate([wide, jnp.zeros((128 - n, 128), jnp.float32)], axis=0)
        st_own[c] = jnp.transpose(wide)[0:8, :]
        for k in range(7):
            remote(st_own.at[c], st_recv.at[c, k], st_r.at[c], (grp_peers[k], t))

    def grad_rows(c, who_core, who_x, who_z):
        n = CHUNKS[c] // 2
        lo = 8 * offs[c] + who_core * 4 * CHUNKS[c] + (who_x * 2 + who_z) * n
        return gbuf.at[pl.ds(pl.multiple_of(lo, 16), n), :]

    def gradient(c):
        n = CHUNKS[c] // 2
        rows = own(c)
        total = st_own[c]
        arrived(st_recv.at[c], st_r.at[c])
        for k in range(7):
            total = total + st_recv[c, k]
        total = jnp.concatenate([total, jnp.zeros((120, 128), jnp.float32)], axis=0)
        total = jnp.transpose(total)[0:n, :]
        s1, s2, s3 = total[:, 0:1], total[:, 1:2], total[:, 2:3]
        inv = lax.rsqrt(s1 / dout + EPS)
        accepted = jnp.sum(counts_v[...].astype(jnp.float32), keepdims=True)
        first = own_rows(c) // SPEC
        sub = lax.broadcasted_iota(jnp.int32, (SPEC, 128), 0)
        live = jnp.concatenate(
            [(sub < counts_s[first + i]).astype(jnp.float32) for i in range(n // SPEC)], axis=0
        )[:, 0:1]
        scale = live / accepted
        gain = gain_ref[...]
        h = hid[rows, :]
        dev = h * inv * gain - tgt[rows, :].astype(jnp.float32)
        res = scale * dev
        coupling = scale * (inv * s2 - s3)
        grad = inv * gain * res - h * (inv * inv * inv * coupling / dout)
        mine = pl.ds(pl.multiple_of(8 * offs[c] + core * 4 * CHUNKS[c] + place * n, 16), n)
        gbuf[mine, :] = grad.astype(jnp.bfloat16)
        ref = gbuf.at[mine, :]
        remote(ref, ref, gz_r.at[c], (g, z_peer))
        for k in range(3):
            remote(ref, ref, gx_r.at[c, k], (g, x_peers[k]))
        remote(ref, ref, gp_r.at[c], (g, other))
        lost = res * dev
        part = loss_acc[...]
        for i in range(n // 8):
            for j in range(cols // 128):
                part = part + lost[8 * i : 8 * i + 8, 128 * j : 128 * j + 128]
        loss_acc[...] = part

    def pass_x(c):
        ref = grad_rows(c, core, x, 1 - zh)
        arrived(ref, gz_r.at[c])
        for k in range(3):
            remote(ref, ref, gx_r.at[c, 3 + k], (g, x_peers[k]))
        remote(ref, ref, gp_r.at[c], (g, other))

    def pass_pair(c, j):
        for k in range(3):
            ref = grad_rows(c, core, x_from[k], zh if j == 0 else 1 - zh)
            arrived(ref, gx_r.at[c, j * 3 + k])
            remote(ref, ref, gp_r.at[c], (g, other))

    def other_grads(c):
        r4 = 4 * CHUNKS[c]
        arrived(gbuf.at[pl.ds(pl.multiple_of(8 * offs[c] + (1 - core) * r4, 16), r4), :], gp_r.at[c])

    n_tiles = depth // TILE
    last = n_chunks - 1

    def outer(i, part):
        if part == 0:
            for c in GROUPS[i]:
                other_grads(c)
        rows = pl.ds(8 * offs[GROUPS[i][0]], 8 * sum(CHUNKS[c] for c in GROUPS[i]))

        def tile(j, _):
            k = pl.ds(pl.multiple_of(j * TILE, TILE), TILE)
            turned = jnp.transpose(fbuf[rows, k])
            for n in range(n_cols):
                col = pl.ds(n * TILE, TILE)
                prod = jnp.dot(turned, gbuf[rows, col], preferred_element_type=jnp.float32)
                if i > 0:
                    prod = prod + acc[k, col]
                if i == len(GROUPS) - 1:
                    out[k, col] = prod.astype(jnp.bfloat16)
                else:
                    acc[k, col] = prod
            return 0

        lax.fori_loop(part * n_tiles // 4, (part + 1) * n_tiles // 4, tile, 0)

    def share_loss():
        for k, p in enumerate(all_tp):
            remote(loss_acc, l1_recv.at[k], l1_r, (g, p))

    def pass_loss():
        total = loss_acc[...]
        arrived(l1_recv, l1_r)
        for k in range(15):
            total = total + l1_recv[k]
        l2_own[...] = total
        for k in range(7):
            remote(l2_own, l2_recv.at[k], l2_r, (grp_peers[k], t))

    loss_acc[...] = jnp.zeros_like(loss_acc)
    steps = {
        "za": own_z_first, "zb": own_z_second, "o1": own_y_first, "o2": own_y_second,
        "r1": round1, "r2": round2, "r3": round3, "r4": round4, "r5": round5, "fin": finish,
        "p": spread_x, "q1": spread_z, "q2": keep_own, "s": stats, "g": gradient, "h": pass_x,
    }
    parted = {"m1": matmul, "x": pass_pair, "d": outer}
    gathering = True
    for step, c, part in ORDER:
        if (step, c, part) == ("m1", 0, 0):
            w_cp.wait()
        if step in parted:
            parted[step](c, part)
        else:
            steps[step](c)
        if (step, c) == ("g", last):
            share_loss()
        if (step, c, part) == ("x", last, 0):
            pass_loss()
        if (step, c) == ("fin", last):
            gathering = False
        for _ in range(4 if gathering else 2):
            if len(sends) > (50 if gathering else 24):
                sends.pop(0).wait_send()
    sum2 = l2_own[...]
    arrived(l2_recv, l2_r)
    for k in range(7):
        sum2 = sum2 + l2_recv[k]
    loss_out[0, 0] = 0.5 * jnp.sum(sum2)
    for cp in sends:
        cp.wait_send()


def shards(features, weight, norm_gain, target, counts):
    rows_g, depth = features.shape
    cols = weight.shape[1]
    total = target.shape[0]
    n = len(CHUNKS)
    bf, f32 = jnp.bfloat16, jnp.float32
    own = total // 16
    dma = pltpu.SemaphoreType.DMA
    anyspace = pl.BlockSpec(memory_space=pl.ANY)
    vmem = pl.BlockSpec(memory_space=pltpu.VMEM)
    unit = depth // 128
    a_units = unit * 14 // 24
    split = (a_units * 128, (a_units // 2) * 128, (unit // 2) * 128)
    out, loss = pl.pallas_call(
        functools.partial(kernel, cols * lax.axis_size("grp"), split),
        out_shape=(
            pltpu.VMEM((depth, cols), bf),
            jax.ShapeDtypeStruct((1, 1), f32),
        ),
        in_specs=[anyspace, anyspace, vmem, anyspace, pl.BlockSpec(memory_space=pltpu.SMEM), vmem],
        out_specs=(vmem, pl.BlockSpec(memory_space=pltpu.SMEM)),
        scratch_shapes=[
            pltpu.VMEM((total, depth), bf),
            pltpu.VMEM((depth, cols), bf),
            pltpu.VMEM((depth, cols), f32),
            pltpu.VMEM((total, cols), bf),
            pltpu.VMEM((total, cols), bf),
            pltpu.VMEM((total // 2, cols), bf),
            pltpu.VMEM((2, 8 * max(CHUNKS), cols), f32),
            pltpu.VMEM((total // 2, cols), bf),
            pltpu.VMEM((2, 3, own, cols), bf),
            pltpu.VMEM((own, cols), bf),
            pltpu.VMEM((own, cols), bf),
            pltpu.VMEM((own, cols), f32),
            pltpu.VMEM((own, cols), bf),
            pltpu.VMEM((n, 8, 128), f32),
            pltpu.VMEM((n, 7, 8, 128), f32),
            pltpu.VMEM((8, 128), f32),
            pltpu.VMEM((15, 8, 128), f32),
            pltpu.VMEM((8, 128), f32),
            pltpu.VMEM((7, 8, 128), f32),
            dma, dma((n,)), dma((n,)), dma((RING,)),
            dma((n, max(AG_SEM) + 1)), dma((n, 2)), dma((n, 2)), dma((n,)), dma((n,)), dma((n,)),
            dma((n, 6)), dma((n,)), dma, dma,
        ],
        compiler_params=pltpu.CompilerParams(
            collective_id=0, has_side_effects=True, vmem_limit_bytes=54 * 1024 * 1024
        ),
    )(features, weight, norm_gain.reshape(1, cols), target, counts, counts.reshape(2, -1))
    return out, loss[0, 0]


def solution(mesh):
    placed = (P("grp", "tp"), P("tp", "grp"), P("grp"), P(None, "grp"), P())
    return jax.shard_map(
        shards, mesh=mesh, in_specs=placed, out_specs=(P("tp", "grp"), P()), check_vma=False
    )
```

```python
import functools

import jax
import jax.numpy as jnp
from jax import lax
from jax.experimental import pallas as pl
from jax.experimental.pallas import tpu as pltpu
from jax.sharding import PartitionSpec as P

SPEC = 8
EPS = 1e-06
CHUNKS = (32, 32, 32, 32, 32, 32, 32, 32)
GROUPS = ((0, 1), (2, 3), (4, 5), (6,), (7,))
ORDER = (
    ("za", 0, 0), ("o1", 0, 0), ("o2", 0, 0), ("zb", 0, 0), ("za", 1, 0), ("o1", 1, 0), ("r2", 0, 0),
    ("r1", 0, 0), ("zb", 1, 0), ("r5", 0, 0), ("r2", 1, 0), ("r1", 1, 0), ("r4", 0, 0), ("za", 2, 0),
    ("r3", 0, 0), ("zb", 2, 0), ("r4", 1, 0), ("o2", 1, 0), ("r3", 1, 0), ("r1", 2, 0), ("za", 3, 0),
    ("fin", 0, 0), ("m1", 0, 0), ("m1", 0, 1), ("r5", 1, 0), ("o1", 2, 0), ("p", 0, 0), ("r1", 3, 0),
    ("zb", 3, 0), ("r3", 2, 0), ("za", 4, 0), ("r2", 2, 0), ("q1", 0, 0), ("fin", 1, 0), ("m1", 1, 0),
    ("r3", 3, 0), ("zb", 4, 0), ("q2", 0, 0), ("m1", 1, 1), ("o2", 2, 0), ("za", 5, 0), ("r1", 4, 0),
    ("p", 1, 0), ("r4", 2, 0), ("s", 0, 0), ("o1", 3, 0), ("zb", 5, 0), ("r5", 2, 0), ("q1", 1, 0),
    ("r1", 5, 0), ("q2", 1, 0), ("r3", 4, 0), ("g", 0, 0), ("r2", 3, 0), ("za", 6, 0), ("r3", 5, 0),
    ("fin", 2, 0), ("x", 0, 0), ("o2", 3, 0), ("zb", 6, 0), ("m1", 2, 0), ("s", 1, 0), ("r4", 3, 0),
    ("h", 0, 0), ("m1", 2, 1), ("r1", 6, 0), ("za", 7, 0), ("p", 2, 0), ("r5", 3, 0), ("o1", 4, 0),
    ("x", 0, 1), ("o2", 4, 0), ("g", 1, 0), ("r3", 6, 0), ("q1", 2, 0), ("r1", 7, 0), ("r2", 4, 0),
    ("q2", 2, 0), ("zb", 7, 0), ("x", 1, 0), ("r5", 4, 0), ("fin", 3, 0), ("m1", 3, 0), ("o1", 5, 0),
    ("h", 1, 0), ("m1", 3, 1), ("r3", 7, 0), ("s", 2, 0), ("p", 3, 0), ("r4", 4, 0), ("o2", 5, 0), ("x", 1, 1),
    ("r2", 5, 0), ("fin", 4, 0), ("q1", 3, 0), ("m1", 4, 0), ("r5", 5, 0), ("o1", 6, 0), ("g", 2, 0),
    ("q2", 3, 0), ("m1", 4, 1), ("r4", 5, 0), ("o2", 6, 0), ("s", 3, 0), ("d", 0, 0), ("o1", 7, 0),
    ("r2", 6, 0), ("x", 2, 0), ("p", 4, 0), ("d", 0, 1), ("r5", 6, 0), ("h", 2, 0), ("d", 0, 2), ("o2", 7, 0),
    ("fin", 5, 0), ("m1", 5, 0), ("r2", 7, 0), ("g", 3, 0), ("q1", 4, 0), ("q2", 4, 0), ("m1", 5, 1),
    ("r4", 6, 0), ("x", 2, 1), ("d", 0, 3), ("r5", 7, 0), ("h", 3, 0), ("x", 3, 0), ("p", 5, 0), ("s", 4, 0),
    ("r4", 7, 0), ("fin", 6, 0), ("m1", 6, 0), ("x", 3, 1), ("m1", 6, 1), ("q1", 5, 0), ("p", 6, 0),
    ("g", 4, 0), ("q2", 5, 0), ("fin", 7, 0), ("m1", 7, 0), ("s", 5, 0), ("m1", 7, 1), ("h", 4, 0),
    ("q1", 6, 0), ("d", 1, 0), ("p", 7, 0), ("x", 4, 0), ("g", 5, 0), ("q2", 6, 0), ("s", 6, 0), ("d", 1, 1),
    ("x", 4, 1), ("d", 1, 2), ("h", 5, 0), ("q1", 7, 0), ("d", 1, 3), ("g", 6, 0), ("q2", 7, 0), ("x", 5, 0),
    ("s", 7, 0), ("x", 5, 1), ("h", 6, 0), ("x", 6, 0), ("g", 7, 0), ("d", 2, 0), ("x", 6, 1), ("d", 2, 1),
    ("h", 7, 0), ("d", 2, 2), ("x", 7, 0), ("d", 2, 3), ("d", 3, 0), ("x", 7, 1), ("d", 3, 1), ("d", 3, 2),
    ("d", 3, 3), ("d", 4, 0), ("d", 4, 1), ("d", 4, 2), ("d", 4, 3),
)
TILE = 256
WIDE = 512
RING = 64
AG_SEM = (0, 1, 2, 3, 4, 5, 6, 7, 8, 8, 3, 3, 3, 9, 10)
MESH = pl.DeviceIdType.MESH

TP_OFF = ((0, 1), (0, 3), (0, 2), (1, 0), (1, 1), (1, 3), (1, 2))
X_OFF = (1, 3, 2)
GRP_OFF = ((0, 1), (1, 0), (3, 0), (2, 0), (1, 1), (3, 1), (2, 1))


def kernel(
    dout, split, features, weight, gain_ref, target, counts_s, counts_v, out, loss_out,
    fbuf, wbuf, acc, gbuf, hsend, hrecv, hfull, hsum, xrecv, zsend, zrecv, hid, tgt,
    st_own, st_recv, loss_acc, l1_recv, l2_own, l2_recv,
    w_sem, f_sem, t_sem, send_sem,
    ag_r, hp_r, rx_r, rz_r, st_r, gz_r, gx_r, gp_r,
    l1_r, l2_r,
):
    g, t = lax.axis_index("grp"), lax.axis_index("tp")
    y, zl = g // 2, lax.rem(g, 2)
    core, q = lax.rem(t, 2), t // 2
    zh, x = q // 4, lax.rem(q, 4)
    depth, cols = wbuf.shape
    rows_g = features.shape[0]
    n_chunks = len(CHUNKS)
    offs = [sum(CHUNKS[:c]) for c in range(n_chunks)]
    a_cols, a_low, half = split
    a_halves = [a_low if c % 2 == 0 else a_cols - a_low for c in range(n_chunks)]
    place = x * 2 + zh

    def grp_dev(dy, dz):
        return lax.rem(y + dy, 4) * 2 + lax.rem(zl + dz, 2)

    def chip(dz, dx):
        return lax.rem(zh + dz, 2) * 4 + lax.rem(x + dx, 4)

    zp, yp, ym, yo = grp_dev(0, 1), grp_dev(1, 0), grp_dev(3, 0), grp_dev(2, 0)
    zyp, zym, zyo = grp_dev(1, 1), grp_dev(3, 1), grp_dev(2, 1)
    other = t + 1 - 2 * core

    tp_peers = [chip(*o) * 2 + core for o in TP_OFF]
    x_peers, z_peer = tp_peers[:3], tp_peers[3]
    x_of = [lax.rem(x + dx, 4) for dx in X_OFF]
    x_from = [lax.rem(x + 4 - dx, 4) for dx in X_OFF]
    grp_peers = [grp_dev(*o) for o in GRP_OFF]
    all_tp = tp_peers + [chip(*o) * 2 + 1 - core for o in TP_OFF] + [other]

    barrier = pltpu.get_barrier_semaphore()
    for p in grp_peers:
        pl.semaphore_signal(barrier, inc=1, device_id=(p, t), device_id_type=MESH)
    for p in all_tp:
        pl.semaphore_signal(barrier, inc=1, device_id=(g, p), device_id_type=MESH)

    sends = []

    sent = [0]

    def remote(src, dst, rsem, dev):
        if len(sends) == RING:
            sends.pop(0).wait_send()
        cp = pltpu.make_async_remote_copy(
            src_ref=src, dst_ref=dst, send_sem=send_sem.at[sent[0] % RING], recv_sem=rsem,
            device_id=dev, device_id_type=MESH,
        )
        cp.start()
        sends.append(cp)
        sent[0] += 1

    def arrived(dst, rsem):
        pltpu.make_async_remote_copy(
            src_ref=dst, dst_ref=dst, send_sem=send_sem.at[0], recv_sem=rsem,
            device_id=(zp, t), device_id_type=MESH,
        ).wait_recv()

    def slot_of(who):
        return lax.rem(who, 2) * 4 + who // 2

    local = []
    for c in range(n_chunks):
        r = CHUNKS[c]
        cp = pltpu.make_async_copy(
            features.at[pl.ds(offs[c], r), :],
            fbuf.at[pl.ds(pl.multiple_of(8 * offs[c] + slot_of(g) * r, 16), r), :],
            f_sem.at[c],
        )
        cp.start()
        local.append(cp)
    w_cp = pltpu.make_async_copy(weight, wbuf, w_sem)
    w_cp.start()

    def own_rows(c):
        r = CHUNKS[c]
        return (x * 2 + core) * rows_g + offs[c] + zh * (r // 2)

    t_cps = []
    for c in range(n_chunks):
        r = CHUNKS[c]
        cp = pltpu.make_async_copy(
            target.at[pl.ds(pl.multiple_of(own_rows(c), 16), r // 2), :],
            tgt.at[pl.ds(offs[c] // 2, r // 2), :],
            t_sem.at[c],
        )
        cp.start()
        t_cps.append(cp)

    pl.semaphore_wait(barrier, len(grp_peers) + len(all_tp))

    def seg(c, who, lo, n):
        r = CHUNKS[c]
        return fbuf.at[pl.ds(pl.multiple_of(8 * offs[c] + slot_of(who) * r, 16), r), pl.ds(lo, n)]

    def ag_put(c, k, who, lo, n, dev):
        remote(seg(c, who, lo, n), seg(c, who, lo, n), ag_r.at[c, AG_SEM[k]], (dev, t))

    def ag_own(c, k, lo, n, dev):
        r = CHUNKS[c]
        remote(
            features.at[pl.ds(offs[c], r), pl.ds(lo, n)], seg(c, g, lo, n),
            ag_r.at[c, AG_SEM[k]], (dev, t),
        )

    def ag_got(c, k, who, lo, n):
        arrived(seg(c, who, lo, n), ag_r.at[c, AG_SEM[k]])

    b_cols = depth - a_cols

    rest = depth - half

    def own_z_first(c):
        ag_own(c, 0, 0, a_cols, zp)

    def own_z_second(c):
        ag_own(c, 3, a_cols, b_cols, zp)

    def own_y_first(c):
        ag_own(c, 1, 0, half, yp)
        ag_own(c, 2, half, rest, ym)

    def own_y_second(c):
        ag_own(c, 13, half, rest, yp)
        ag_own(c, 14, 0, half, ym)

    def round1(c):
        ag_got(c, 0, zp, 0, a_cols)
        ag_put(c, 4, zp, 0, a_cols, yp)
        ag_put(c, 5, zp, 0, a_cols, ym)

    def round2(c):
        ag_got(c, 1, ym, 0, half)
        ag_put(c, 6, ym, 0, half, yp)
        ag_got(c, 2, yp, half, rest)
        ag_put(c, 7, yp, half, rest, ym)

    def round3(c):
        ag_got(c, 4, zym, 0, a_cols)
        ag_put(c, 8, zym, 0, a_halves[c], yp)
        ag_got(c, 5, zyp, 0, a_cols)
        ag_put(c, 9, zyp, a_halves[c], a_cols - a_halves[c], ym)

    def round4(c):
        ag_got(c, 7, yo, half, rest)
        ag_put(c, 12, yo, a_cols, b_cols, zp)

    def round5(c):
        ag_got(c, 13, ym, half, rest)
        ag_put(c, 10, ym, a_cols, b_cols, zp)
        ag_put(c, 11, yp, a_cols, b_cols, zp)

    def finish(c):
        r = CHUNKS[c]
        ag_got(c, 6, yo, 0, half)
        ag_got(c, 14, yp, 0, half)
        ag_got(c, 8, zyo, 0, a_cols)
        plane = pl.ds(pl.multiple_of(8 * offs[c] + (1 - zl) * 4 * r, 16), 4 * r)
        arrived(fbuf.at[plane, pl.ds(a_cols, b_cols)], ag_r.at[c, AG_SEM[3]])
        local[c].wait()

    n_cols = cols // TILE
    parts = 2

    def matmul(c, part):
        r8 = 8 * CHUNKS[c]
        rows = pl.ds(8 * offs[c], r8)

        def tile(n, _):
            col = pl.ds(pl.multiple_of(n * TILE, TILE), TILE)
            prod = jnp.dot(fbuf[rows, :], wbuf[:, col], preferred_element_type=jnp.float32)
            hfull[c % 2, pl.ds(0, r8), col] = prod
            hsend[rows, col] = prod.astype(jnp.bfloat16)
            return 0

        lax.fori_loop(part * n_cols // parts, (part + 1) * n_cols // parts, tile, 0)
        wide = pl.ds(part * cols // parts, cols // parts)
        theirs = pl.ds(pl.multiple_of(8 * offs[c] + (1 - core) * (r8 // 2), 16), r8 // 2)
        remote(
            hsend.at[theirs, wide], hrecv.at[pl.ds(4 * offs[c], r8 // 2), wide],
            hp_r.at[c, part], (g, other),
        )

    def mine(c, lo, n):
        return c % 2, pl.ds(pl.multiple_of(core * 4 * CHUNKS[c] + lo, 16), n)

    def own(c):
        return pl.ds(offs[c] // 2, CHUNKS[c] // 2)

    def spread_x(c):
        r = CHUNKS[c]
        base, n = 4 * offs[c], r // 2
        for i in range(parts):
            wide = pl.ds(i * cols // parts, cols // parts)
            arrived(hrecv.at[pl.ds(base, 4 * r), wide], hp_r.at[c, i])

        def add(i, _):
            lo = pl.multiple_of(i * 16, 16)
            slot, rows = mine(c, lo, 16)
            both = hfull[slot, rows, :] + hrecv[pl.ds(base + lo, 16), :].astype(jnp.float32)
            hfull[slot, rows, :] = both
            hsum[pl.ds(base + lo, 16), :] = both.astype(jnp.bfloat16)
            return 0

        lax.fori_loop(0, 4 * r // 16, add, 0)
        for j in range(2):
            for k in range(3):
                z = 1 - zh if j == 0 else zh
                remote(
                    hsum.at[pl.ds(pl.multiple_of(base + (x_of[k] * 2 + z) * n, 16), n), :],
                    xrecv.at[j, k, own(c), :],
                    rx_r.at[c, j], (g, x_peers[k]),
                )

    def sum_x(c, j):
        n = CHUNKS[c] // 2
        z = 1 - zh if j == 0 else zh
        arrived(xrecv.at[j, :, own(c), :], rx_r.at[c, j])
        slot, rows = mine(c, (x * 2 + z) * n, n)
        h = hfull[slot, rows, :]
        for k in range(3):
            h = h + xrecv[j, k, own(c), :].astype(jnp.float32)
        return h

    def spread_z(c):
        zsend[own(c), :] = sum_x(c, 0).astype(jnp.bfloat16)
        remote(zsend.at[own(c), :], zrecv.at[own(c), :], rz_r.at[c], (g, z_peer))

    def keep_own(c):
        hid[own(c), :] = sum_x(c, 1)

    def stats(c):
        n = CHUNKS[c] // 2
        rows = own(c)
        arrived(zrecv.at[rows, :], rz_r.at[c])
        h = hid[rows, :] + zrecv[rows, :].astype(jnp.float32)
        hid[rows, :] = h
        t_cps[c].wait()
        gh = gain_ref[...] * h
        s1 = jnp.sum(h * h, axis=1, keepdims=True)
        s2 = jnp.sum(gh * gh, axis=1, keepdims=True)
        s3 = jnp.sum(gh * tgt[rows, :].astype(jnp.float32), axis=1, keepdims=True)
        lane = lax.broadcasted_iota(jnp.int32, (n, 128), 1)
        wide = jnp.where(lane == 0, s1, jnp.where(lane == 1, s2, s3))
        wide = jnp.concatenate([wide, jnp.zeros((128 - n, 128), jnp.float32)], axis=0)
        st_own[c] = jnp.transpose(wide)[0:8, :]
        for k in range(7):
            remote(st_own.at[c], st_recv.at[c, k], st_r.at[c], (grp_peers[k], t))

    def grad_rows(c, who_core, who_x, who_z):
        n = CHUNKS[c] // 2
        lo = 8 * offs[c] + who_core * 4 * CHUNKS[c] + (who_x * 2 + who_z) * n
        return gbuf.at[pl.ds(pl.multiple_of(lo, 16), n), :]

    def gradient(c):
        n = CHUNKS[c] // 2
        rows = own(c)
        total = st_own[c]
        arrived(st_recv.at[c], st_r.at[c])
        for k in range(7):
            total = total + st_recv[c, k]
        total = jnp.concatenate([total, jnp.zeros((120, 128), jnp.float32)], axis=0)
        total = jnp.transpose(total)[0:n, :]
        s1, s2, s3 = total[:, 0:1], total[:, 1:2], total[:, 2:3]
        inv = lax.rsqrt(s1 / dout + EPS)
        accepted = jnp.sum(counts_v[...].astype(jnp.float32), keepdims=True)
        first = own_rows(c) // SPEC
        sub = lax.broadcasted_iota(jnp.int32, (SPEC, 128), 0)
        live = jnp.concatenate(
            [(sub < counts_s[first + i]).astype(jnp.float32) for i in range(n // SPEC)], axis=0
        )[:, 0:1]
        scale = live / accepted
        gain = gain_ref[...]
        h = hid[rows, :]
        dev = h * inv * gain - tgt[rows, :].astype(jnp.float32)
        res = scale * dev
        coupling = scale * (inv * s2 - s3)
        grad = inv * gain * res - h * (inv * inv * inv * coupling / dout)
        mine = pl.ds(pl.multiple_of(8 * offs[c] + core * 4 * CHUNKS[c] + place * n, 16), n)
        gbuf[mine, :] = grad.astype(jnp.bfloat16)
        ref = gbuf.at[mine, :]
        remote(ref, ref, gz_r.at[c], (g, z_peer))
        for k in range(3):
            remote(ref, ref, gx_r.at[c, k], (g, x_peers[k]))
        remote(ref, ref, gp_r.at[c], (g, other))
        lost = res * dev
        part = loss_acc[...]
        for i in range(n // 8):
            for j in range(cols // 128):
                part = part + lost[8 * i : 8 * i + 8, 128 * j : 128 * j + 128]
        loss_acc[...] = part

    def pass_x(c):
        ref = grad_rows(c, core, x, 1 - zh)
        arrived(ref, gz_r.at[c])
        for k in range(3):
            remote(ref, ref, gx_r.at[c, 3 + k], (g, x_peers[k]))
        remote(ref, ref, gp_r.at[c], (g, other))

    def pass_pair(c, j):
        for k in range(3):
            ref = grad_rows(c, core, x_from[k], zh if j == 0 else 1 - zh)
            arrived(ref, gx_r.at[c, j * 3 + k])
            remote(ref, ref, gp_r.at[c], (g, other))

    def other_grads(c):
        r4 = 4 * CHUNKS[c]
        arrived(gbuf.at[pl.ds(pl.multiple_of(8 * offs[c] + (1 - core) * r4, 16), r4), :], gp_r.at[c])

    n_tiles = depth // WIDE
    last = n_chunks - 1

    def outer(i, part):
        if part == 0:
            for c in GROUPS[i]:
                other_grads(c)
        rows = pl.ds(8 * offs[GROUPS[i][0]], 8 * sum(CHUNKS[c] for c in GROUPS[i]))

        def tile(j, _):
            k = pl.ds(pl.multiple_of(j * WIDE, WIDE), WIDE)
            turned = jnp.transpose(fbuf[rows, k])
            for n in range(n_cols):
                col = pl.ds(n * TILE, TILE)
                prod = jnp.dot(turned, gbuf[rows, col], preferred_element_type=jnp.float32)
                if i > 0:
                    prod = prod + acc[k, col]
                if i == len(GROUPS) - 1:
                    out[k, col] = prod.astype(jnp.bfloat16)
                else:
                    acc[k, col] = prod
            return 0

        lax.fori_loop(part * n_tiles // 4, (part + 1) * n_tiles // 4, tile, 0)

    def share_loss():
        for k, p in enumerate(all_tp):
            remote(loss_acc, l1_recv.at[k], l1_r, (g, p))

    def pass_loss():
        total = loss_acc[...]
        arrived(l1_recv, l1_r)
        for k in range(15):
            total = total + l1_recv[k]
        l2_own[...] = total
        for k in range(7):
            remote(l2_own, l2_recv.at[k], l2_r, (grp_peers[k], t))

    loss_acc[...] = jnp.zeros_like(loss_acc)
    steps = {
        "za": own_z_first, "zb": own_z_second, "o1": own_y_first, "o2": own_y_second,
        "r1": round1, "r2": round2, "r3": round3, "r4": round4, "r5": round5, "fin": finish,
        "p": spread_x, "q1": spread_z, "q2": keep_own, "s": stats, "g": gradient, "h": pass_x,
    }
    parted = {"m1": matmul, "x": pass_pair, "d": outer}
    gathering = True
    for step, c, part in ORDER:
        if (step, c, part) == ("m1", 0, 0):
            w_cp.wait()
        if step in parted:
            parted[step](c, part)
        else:
            steps[step](c)
        if (step, c) == ("g", last):
            share_loss()
        if (step, c, part) == ("x", last, 0):
            pass_loss()
        if (step, c) == ("fin", last):
            gathering = False
        for _ in range(4 if gathering else 2):
            if len(sends) > (50 if gathering else 24):
                sends.pop(0).wait_send()
    sum2 = l2_own[...]
    arrived(l2_recv, l2_r)
    for k in range(7):
        sum2 = sum2 + l2_recv[k]
    loss_out[0, 0] = 0.5 * jnp.sum(sum2)
    for cp in sends:
        cp.wait_send()


def shards(features, weight, norm_gain, target, counts):
    rows_g, depth = features.shape
    cols = weight.shape[1]
    total = target.shape[0]
    n = len(CHUNKS)
    bf, f32 = jnp.bfloat16, jnp.float32
    own = total // 16
    dma = pltpu.SemaphoreType.DMA
    anyspace = pl.BlockSpec(memory_space=pl.ANY)
    vmem = pl.BlockSpec(memory_space=pltpu.VMEM)
    unit = depth // 128
    a_units = unit * 14 // 24
    split = (a_units * 128, (a_units // 2) * 128, (unit // 2) * 128)
    out, loss = pl.pallas_call(
        functools.partial(kernel, cols * lax.axis_size("grp"), split),
        out_shape=(
            pltpu.VMEM((depth, cols), bf),
            jax.ShapeDtypeStruct((1, 1), f32),
        ),
        in_specs=[anyspace, anyspace, vmem, anyspace, pl.BlockSpec(memory_space=pltpu.SMEM), vmem],
        out_specs=(vmem, pl.BlockSpec(memory_space=pltpu.SMEM)),
        scratch_shapes=[
            pltpu.VMEM((total, depth), bf),
            pltpu.VMEM((depth, cols), bf),
            pltpu.VMEM((depth, cols), f32),
            pltpu.VMEM((total, cols), bf),
            pltpu.VMEM((total, cols), bf),
            pltpu.VMEM((total // 2, cols), bf),
            pltpu.VMEM((2, 8 * max(CHUNKS), cols), f32),
            pltpu.VMEM((total // 2, cols), bf),
            pltpu.VMEM((2, 3, own, cols), bf),
            pltpu.VMEM((own, cols), bf),
            pltpu.VMEM((own, cols), bf),
            pltpu.VMEM((own, cols), f32),
            pltpu.VMEM((own, cols), bf),
            pltpu.VMEM((n, 8, 128), f32),
            pltpu.VMEM((n, 7, 8, 128), f32),
            pltpu.VMEM((8, 128), f32),
            pltpu.VMEM((15, 8, 128), f32),
            pltpu.VMEM((8, 128), f32),
            pltpu.VMEM((7, 8, 128), f32),
            dma, dma((n,)), dma((n,)), dma((RING,)),
            dma((n, max(AG_SEM) + 1)), dma((n, 2)), dma((n, 2)), dma((n,)), dma((n,)), dma((n,)),
            dma((n, 6)), dma((n,)), dma, dma,
        ],
        compiler_params=pltpu.CompilerParams(
            collective_id=0, has_side_effects=True, vmem_limit_bytes=54 * 1024 * 1024
        ),
    )(features, weight, norm_gain.reshape(1, cols), target, counts, counts.reshape(2, -1))
    return out, loss[0, 0]


def solution(mesh):
    placed = (P("grp", "tp"), P("tp", "grp"), P("grp"), P(None, "grp"), P())
    return jax.shard_map(
        shards, mesh=mesh, in_specs=placed, out_specs=(P("tp", "grp"), P()), check_vma=False
    )
```

```python
import functools

import jax
import jax.numpy as jnp
from jax import lax
from jax.experimental import pallas as pl
from jax.experimental.pallas import tpu as pltpu
from jax.sharding import PartitionSpec as P

SPEC = 8
EPS = 1e-06
CHUNKS = (32, 32, 32, 32, 32, 32, 32, 32)
GROUPS = ((0, 1), (2, 3), (4, 5), (6,), (7,))
ORDER = (
    ("za", 0, 0), ("o1", 0, 0), ("o2", 0, 0), ("zb", 0, 0), ("za", 1, 0), ("o1", 1, 0), ("r2", 0, 0),
    ("r1", 0, 0), ("zb", 1, 0), ("r5", 0, 0), ("r2", 1, 0), ("r1", 1, 0), ("r4", 0, 0), ("za", 2, 0),
    ("r3", 0, 0), ("zb", 2, 0), ("r4", 1, 0), ("o2", 1, 0), ("r3", 1, 0), ("r1", 2, 0), ("za", 3, 0),
    ("fin", 0, 0), ("m1", 0, 0), ("m1", 0, 1), ("r5", 1, 0), ("o1", 2, 0), ("p", 0, 0), ("r1", 3, 0),
    ("zb", 3, 0), ("r3", 2, 0), ("za", 4, 0), ("r2", 2, 0), ("q1", 0, 0), ("fin", 1, 0), ("m1", 1, 0),
    ("r3", 3, 0), ("zb", 4, 0), ("q2", 0, 0), ("m1", 1, 1), ("o2", 2, 0), ("za", 5, 0), ("r1", 4, 0),
    ("p", 1, 0), ("r4", 2, 0), ("s", 0, 0), ("o1", 3, 0), ("zb", 5, 0), ("r5", 2, 0), ("q1", 1, 0),
    ("r1", 5, 0), ("q2", 1, 0), ("r3", 4, 0), ("g", 0, 0), ("r2", 3, 0), ("za", 6, 0), ("r3", 5, 0),
    ("fin", 2, 0), ("x", 0, 0), ("o2", 3, 0), ("zb", 6, 0), ("m1", 2, 0), ("s", 1, 0), ("r4", 3, 0),
    ("h", 0, 0), ("m1", 2, 1), ("r1", 6, 0), ("za", 7, 0), ("p", 2, 0), ("r5", 3, 0), ("o1", 4, 0),
    ("x", 0, 1), ("o2", 4, 0), ("g", 1, 0), ("r3", 6, 0), ("q1", 2, 0), ("r1", 7, 0), ("r2", 4, 0),
    ("q2", 2, 0), ("zb", 7, 0), ("x", 1, 0), ("r5", 4, 0), ("fin", 3, 0), ("m1", 3, 0), ("o1", 5, 0),
    ("h", 1, 0), ("m1", 3, 1), ("r3", 7, 0), ("s", 2, 0), ("p", 3, 0), ("r4", 4, 0), ("o2", 5, 0), ("x", 1, 1),
    ("r2", 5, 0), ("fin", 4, 0), ("q1", 3, 0), ("m1", 4, 0), ("r5", 5, 0), ("o1", 6, 0), ("g", 2, 0),
    ("q2", 3, 0), ("m1", 4, 1), ("r4", 5, 0), ("o2", 6, 0), ("s", 3, 0), ("d", 0, 0), ("o1", 7, 0),
    ("r2", 6, 0), ("x", 2, 0), ("p", 4, 0), ("d", 0, 1), ("r5", 6, 0), ("h", 2, 0), ("d", 0, 2), ("o2", 7, 0),
    ("fin", 5, 0), ("m1", 5, 0), ("r2", 7, 0), ("g", 3, 0), ("q1", 4, 0), ("q2", 4, 0), ("m1", 5, 1),
    ("r4", 6, 0), ("x", 2, 1), ("d", 0, 3), ("r5", 7, 0), ("h", 3, 0), ("x", 3, 0), ("p", 5, 0), ("s", 4, 0),
    ("r4", 7, 0), ("fin", 6, 0), ("m1", 6, 0), ("x", 3, 1), ("m1", 6, 1), ("q1", 5, 0), ("p", 6, 0),
    ("g", 4, 0), ("q2", 5, 0), ("fin", 7, 0), ("m1", 7, 0), ("s", 5, 0), ("m1", 7, 1), ("h", 4, 0),
    ("q1", 6, 0), ("d", 1, 0), ("p", 7, 0), ("x", 4, 0), ("g", 5, 0), ("q2", 6, 0), ("s", 6, 0), ("d", 1, 1),
    ("x", 4, 1), ("d", 1, 2), ("h", 5, 0), ("q1", 7, 0), ("d", 1, 3), ("g", 6, 0), ("q2", 7, 0), ("x", 5, 0),
    ("s", 7, 0), ("x", 5, 1), ("h", 6, 0), ("x", 6, 0), ("g", 7, 0), ("d", 2, 0), ("x", 6, 1), ("d", 2, 1),
    ("h", 7, 0), ("d", 2, 2), ("x", 7, 0), ("d", 2, 3), ("d", 3, 0), ("x", 7, 1), ("d", 3, 1), ("d", 3, 2),
    ("d", 3, 3), ("d", 4, 0), ("d", 4, 1), ("d", 4, 2), ("d", 4, 3),
)
TILE = 256
WIDE = 512
RING = 64
AG_SEM = (0, 1, 2, 3, 4, 5, 6, 7, 8, 8, 3, 3, 3, 9, 10)
MESH = pl.DeviceIdType.MESH

TP_OFF = ((0, 1), (0, 3), (0, 2), (1, 0), (1, 1), (1, 3), (1, 2))
X_OFF = (1, 3, 2)
GRP_OFF = ((0, 1), (1, 0), (3, 0), (2, 0), (1, 1), (3, 1), (2, 1))


def kernel(
    dout, split, features, weight, gain_ref, target, counts_s, counts_v, out, loss_out,
    fbuf, wbuf, acc, gbuf, hsend, hrecv, hfull, hsum, xrecv, zsend, zrecv, hid, tgt,
    st_own, st_recv, loss_acc, l1_recv, l2_own, l2_recv,
    w_sem, f_sem, t_sem, send_sem,
    ag_r, hp_r, rx_r, rz_r, st_r, gz_r, gx_r, gp_r,
    l1_r, l2_r,
):
    g, t = lax.axis_index("grp"), lax.axis_index("tp")
    y, zl = g // 2, lax.rem(g, 2)
    core, q = lax.rem(t, 2), t // 2
    zh, x = q // 4, lax.rem(q, 4)
    depth, cols = wbuf.shape
    rows_g = features.shape[0]
    n_chunks = len(CHUNKS)
    offs = [sum(CHUNKS[:c]) for c in range(n_chunks)]
    a_cols, a_low, half = split
    a_halves = [a_low if c % 2 == 0 else a_cols - a_low for c in range(n_chunks)]
    place = x * 2 + zh

    def grp_dev(dy, dz):
        return lax.rem(y + dy, 4) * 2 + lax.rem(zl + dz, 2)

    def chip(dz, dx):
        return lax.rem(zh + dz, 2) * 4 + lax.rem(x + dx, 4)

    zp, yp, ym, yo = grp_dev(0, 1), grp_dev(1, 0), grp_dev(3, 0), grp_dev(2, 0)
    zyp, zym, zyo = grp_dev(1, 1), grp_dev(3, 1), grp_dev(2, 1)
    other = t + 1 - 2 * core

    tp_peers = [chip(*o) * 2 + core for o in TP_OFF]
    x_peers, z_peer = tp_peers[:3], tp_peers[3]
    x_of = [lax.rem(x + dx, 4) for dx in X_OFF]
    x_from = [lax.rem(x + 4 - dx, 4) for dx in X_OFF]
    grp_peers = [grp_dev(*o) for o in GRP_OFF]
    all_tp = tp_peers + [chip(*o) * 2 + 1 - core for o in TP_OFF] + [other]

    barrier = pltpu.get_barrier_semaphore()
    for p in grp_peers:
        pl.semaphore_signal(barrier, inc=1, device_id=(p, t), device_id_type=MESH)
    for p in all_tp:
        pl.semaphore_signal(barrier, inc=1, device_id=(g, p), device_id_type=MESH)

    sends = []

    sent = [0]

    def remote(src, dst, rsem, dev):
        if len(sends) == RING:
            sends.pop(0).wait_send()
        cp = pltpu.make_async_remote_copy(
            src_ref=src, dst_ref=dst, send_sem=send_sem.at[sent[0] % RING], recv_sem=rsem,
            device_id=dev, device_id_type=MESH,
        )
        cp.start()
        sends.append(cp)
        sent[0] += 1

    def arrived(dst, rsem):
        pltpu.make_async_remote_copy(
            src_ref=dst, dst_ref=dst, send_sem=send_sem.at[0], recv_sem=rsem,
            device_id=(zp, t), device_id_type=MESH,
        ).wait_recv()

    def slot_of(who):
        return lax.rem(who, 2) * 4 + who // 2

    local = []
    for c in range(n_chunks):
        r = CHUNKS[c]
        cp = pltpu.make_async_copy(
            features.at[pl.ds(offs[c], r), :],
            fbuf.at[pl.ds(pl.multiple_of(8 * offs[c] + slot_of(g) * r, 16), r), :],
            f_sem.at[c],
        )
        cp.start()
        local.append(cp)
    w_cp = pltpu.make_async_copy(weight, wbuf, w_sem)
    w_cp.start()

    def own_rows(c):
        r = CHUNKS[c]
        return (x * 2 + core) * rows_g + offs[c] + zh * (r // 2)

    t_cps = []
    for c in range(n_chunks):
        r = CHUNKS[c]
        cp = pltpu.make_async_copy(
            target.at[pl.ds(pl.multiple_of(own_rows(c), 16), r // 2), :],
            tgt.at[pl.ds(offs[c] // 2, r // 2), :],
            t_sem.at[c],
        )
        cp.start()
        t_cps.append(cp)

    pl.semaphore_wait(barrier, len(grp_peers) + len(all_tp))

    def seg(c, who, lo, n):
        r = CHUNKS[c]
        return fbuf.at[pl.ds(pl.multiple_of(8 * offs[c] + slot_of(who) * r, 16), r), pl.ds(lo, n)]

    def ag_put(c, k, who, lo, n, dev):
        remote(seg(c, who, lo, n), seg(c, who, lo, n), ag_r.at[c, AG_SEM[k]], (dev, t))

    def ag_own(c, k, lo, n, dev):
        r = CHUNKS[c]
        remote(
            features.at[pl.ds(offs[c], r), pl.ds(lo, n)], seg(c, g, lo, n),
            ag_r.at[c, AG_SEM[k]], (dev, t),
        )

    def ag_got(c, k, who, lo, n):
        arrived(seg(c, who, lo, n), ag_r.at[c, AG_SEM[k]])

    b_cols = depth - a_cols

    rest = depth - half

    def own_z_first(c):
        ag_own(c, 0, 0, a_cols, zp)

    def own_z_second(c):
        ag_own(c, 3, a_cols, b_cols, zp)

    def own_y_first(c):
        ag_own(c, 1, 0, half, yp)
        ag_own(c, 2, half, rest, ym)

    def own_y_second(c):
        ag_own(c, 13, half, rest, yp)
        ag_own(c, 14, 0, half, ym)

    def round1(c):
        ag_got(c, 0, zp, 0, a_cols)
        ag_put(c, 4, zp, 0, a_cols, yp)
        ag_put(c, 5, zp, 0, a_cols, ym)

    def round2(c):
        ag_got(c, 1, ym, 0, half)
        ag_put(c, 6, ym, 0, half, yp)
        ag_got(c, 2, yp, half, rest)
        ag_put(c, 7, yp, half, rest, ym)

    def round3(c):
        ag_got(c, 4, zym, 0, a_cols)
        ag_put(c, 8, zym, 0, a_halves[c], yp)
        ag_got(c, 5, zyp, 0, a_cols)
        ag_put(c, 9, zyp, a_halves[c], a_cols - a_halves[c], ym)

    def round4(c):
        ag_got(c, 7, yo, half, rest)
        ag_put(c, 12, yo, a_cols, b_cols, zp)

    def round5(c):
        ag_got(c, 13, ym, half, rest)
        ag_put(c, 10, ym, a_cols, b_cols, zp)
        ag_put(c, 11, yp, a_cols, b_cols, zp)

    def finish(c):
        r = CHUNKS[c]
        ag_got(c, 6, yo, 0, half)
        ag_got(c, 14, yp, 0, half)
        ag_got(c, 8, zyo, 0, a_cols)
        plane = pl.ds(pl.multiple_of(8 * offs[c] + (1 - zl) * 4 * r, 16), 4 * r)
        arrived(fbuf.at[plane, pl.ds(a_cols, b_cols)], ag_r.at[c, AG_SEM[3]])
        local[c].wait()

    n_cols = cols // TILE
    parts = 2

    def matmul(c, part):
        r8 = 8 * CHUNKS[c]
        rows = pl.ds(8 * offs[c], r8)

        def tile(n, _):
            col = pl.ds(pl.multiple_of(n * TILE, TILE), TILE)
            prod = jnp.dot(fbuf[rows, :], wbuf[:, col], preferred_element_type=jnp.float32)
            hfull[c % 2, pl.ds(0, r8), col] = prod
            hsend[rows, col] = prod.astype(jnp.bfloat16)
            return 0

        lax.fori_loop(part * n_cols // parts, (part + 1) * n_cols // parts, tile, 0)
        wide = pl.ds(part * cols // parts, cols // parts)
        theirs = pl.ds(pl.multiple_of(8 * offs[c] + (1 - core) * (r8 // 2), 16), r8 // 2)
        remote(
            hsend.at[theirs, wide], hrecv.at[pl.ds(4 * offs[c], r8 // 2), wide],
            hp_r.at[c, part], (g, other),
        )

    def mine(c, lo, n):
        return c % 2, pl.ds(pl.multiple_of(core * 4 * CHUNKS[c] + lo, 16), n)

    def own(c):
        return pl.ds(offs[c] // 2, CHUNKS[c] // 2)

    def spread_x(c):
        r = CHUNKS[c]
        base, n = 4 * offs[c], r // 2
        for i in range(parts):
            wide = pl.ds(i * cols // parts, cols // parts)
            arrived(hrecv.at[pl.ds(base, 4 * r), wide], hp_r.at[c, i])

        def add(i, _):
            lo = pl.multiple_of(i * 16, 16)
            slot, rows = mine(c, lo, 16)
            both = hfull[slot, rows, :] + hrecv[pl.ds(base + lo, 16), :].astype(jnp.float32)
            hfull[slot, rows, :] = both
            hsum[pl.ds(base + lo, 16), :] = both.astype(jnp.bfloat16)
            return 0

        lax.fori_loop(0, 4 * r // 16, add, 0)
        for j in range(2):
            for k in range(3):
                z = 1 - zh if j == 0 else zh
                remote(
                    hsum.at[pl.ds(pl.multiple_of(base + (x_of[k] * 2 + z) * n, 16), n), :],
                    xrecv.at[j, k, own(c), :],
                    rx_r.at[c, j], (g, x_peers[k]),
                )

    def sum_x(c, j):
        n = CHUNKS[c] // 2
        z = 1 - zh if j == 0 else zh
        arrived(xrecv.at[j, :, own(c), :], rx_r.at[c, j])
        slot, rows = mine(c, (x * 2 + z) * n, n)
        h = hfull[slot, rows, :]
        for k in range(3):
            h = h + xrecv[j, k, own(c), :].astype(jnp.float32)
        return h

    def spread_z(c):
        zsend[own(c), :] = sum_x(c, 0).astype(jnp.bfloat16)
        remote(zsend.at[own(c), :], zrecv.at[own(c), :], rz_r.at[c], (g, z_peer))

    def keep_own(c):
        hid[own(c), :] = sum_x(c, 1)

    def stats(c):
        n = CHUNKS[c] // 2
        rows = own(c)
        arrived(zrecv.at[rows, :], rz_r.at[c])
        h = hid[rows, :] + zrecv[rows, :].astype(jnp.float32)
        hid[rows, :] = h
        t_cps[c].wait()
        gh = gain_ref[...] * h
        s1 = jnp.sum(h * h, axis=1, keepdims=True)
        s2 = jnp.sum(gh * gh, axis=1, keepdims=True)
        s3 = jnp.sum(gh * tgt[rows, :].astype(jnp.float32), axis=1, keepdims=True)
        lane = lax.broadcasted_iota(jnp.int32, (n, 128), 1)
        wide = jnp.where(lane == 0, s1, jnp.where(lane == 1, s2, s3))
        wide = jnp.concatenate([wide, jnp.zeros((128 - n, 128), jnp.float32)], axis=0)
        st_own[c] = jnp.transpose(wide)[0:8, :]
        for k in range(7):
            remote(st_own.at[c], st_recv.at[c, k], st_r.at[c], (grp_peers[k], t))

    def grad_rows(c, who_core, who_x, who_z):
        n = CHUNKS[c] // 2
        lo = 8 * offs[c] + who_core * 4 * CHUNKS[c] + (who_x * 2 + who_z) * n
        return gbuf.at[pl.ds(pl.multiple_of(lo, 16), n), :]

    def gradient(c):
        n = CHUNKS[c] // 2
        rows = own(c)
        total = st_own[c]
        arrived(st_recv.at[c], st_r.at[c])
        for k in range(7):
            total = total + st_recv[c, k]
        total = jnp.concatenate([total, jnp.zeros((120, 128), jnp.float32)], axis=0)
        total = jnp.transpose(total)[0:n, :]
        s1, s2, s3 = total[:, 0:1], total[:, 1:2], total[:, 2:3]
        inv = lax.rsqrt(s1 / dout + EPS)
        accepted = jnp.sum(counts_v[...].astype(jnp.float32), keepdims=True)
        first = own_rows(c) // SPEC
        sub = lax.broadcasted_iota(jnp.int32, (SPEC, 128), 0)
        live = jnp.concatenate(
            [(sub < counts_s[first + i]).astype(jnp.float32) for i in range(n // SPEC)], axis=0
        )[:, 0:1]
        scale = live / accepted
        gain = gain_ref[...]
        h = hid[rows, :]
        dev = h * inv * gain - tgt[rows, :].astype(jnp.float32)
        res = scale * dev
        coupling = scale * (inv * s2 - s3)
        grad = inv * gain * res - h * (inv * inv * inv * coupling / dout)
        mine = pl.ds(pl.multiple_of(8 * offs[c] + core * 4 * CHUNKS[c] + place * n, 16), n)
        gbuf[mine, :] = grad.astype(jnp.bfloat16)
        ref = gbuf.at[mine, :]
        remote(ref, ref, gz_r.at[c], (g, z_peer))
        for k in range(3):
            remote(ref, ref, gx_r.at[c, k], (g, x_peers[k]))
        remote(ref, ref, gp_r.at[c], (g, other))
        lost = res * dev
        part = loss_acc[...]
        for i in range(n // 8):
            for j in range(cols // 128):
                part = part + lost[8 * i : 8 * i + 8, 128 * j : 128 * j + 128]
        loss_acc[...] = part

    def pass_x(c):
        ref = grad_rows(c, core, x, 1 - zh)
        arrived(ref, gz_r.at[c])
        for k in range(3):
            remote(ref, ref, gx_r.at[c, 3 + k], (g, x_peers[k]))
        remote(ref, ref, gp_r.at[c], (g, other))

    def pass_pair(c, j):
        for k in range(3):
            ref = grad_rows(c, core, x_from[k], zh if j == 0 else 1 - zh)
            arrived(ref, gx_r.at[c, j * 3 + k])
            remote(ref, ref, gp_r.at[c], (g, other))

    def other_grads(c):
        r4 = 4 * CHUNKS[c]
        arrived(gbuf.at[pl.ds(pl.multiple_of(8 * offs[c] + (1 - core) * r4, 16), r4), :], gp_r.at[c])

    n_tiles = depth // WIDE
    last = n_chunks - 1

    def outer(i, part):
        if part == 0:
            for c in GROUPS[i]:
                other_grads(c)
        rows = pl.ds(8 * offs[GROUPS[i][0]], 8 * sum(CHUNKS[c] for c in GROUPS[i]))

        def tile(j, _):
            k = pl.ds(pl.multiple_of(j * WIDE, WIDE), WIDE)
            turned = jnp.transpose(fbuf[rows, k])
            for n in range(n_cols):
                col = pl.ds(n * TILE, TILE)
                prod = jnp.dot(turned, gbuf[rows, col], preferred_element_type=jnp.float32)
                if i > 0:
                    prod = prod + acc[k, col]
                if i == len(GROUPS) - 1:
                    out[k, col] = prod.astype(jnp.bfloat16)
                else:
                    acc[k, col] = prod
            return 0

        lax.fori_loop(part * n_tiles // 4, (part + 1) * n_tiles // 4, tile, 0)

    def share_loss():
        for k, p in enumerate(all_tp):
            remote(loss_acc, l1_recv.at[k], l1_r, (g, p))

    def pass_loss():
        total = loss_acc[...]
        arrived(l1_recv, l1_r)
        for k in range(15):
            total = total + l1_recv[k]
        l2_own[...] = total
        for k in range(7):
            remote(l2_own, l2_recv.at[k], l2_r, (grp_peers[k], t))

    loss_acc[...] = jnp.zeros_like(loss_acc)
    steps = {
        "za": own_z_first, "zb": own_z_second, "o1": own_y_first, "o2": own_y_second,
        "r1": round1, "r2": round2, "r3": round3, "r4": round4, "r5": round5, "fin": finish,
        "p": spread_x, "q1": spread_z, "q2": keep_own, "s": stats, "g": gradient, "h": pass_x,
    }
    parted = {"m1": matmul, "x": pass_pair, "d": outer}
    gathering = True
    for step, c, part in ORDER:
        if (step, c, part) == ("m1", 0, 0):
            w_cp.wait()
        if (step, c, part) == ("d", len(GROUPS) - 1, 0):
            pass_loss()
        if step in parted:
            parted[step](c, part)
        else:
            steps[step](c)
        if (step, c) == ("g", last):
            share_loss()
        if (step, c) == ("fin", last):
            gathering = False
        for _ in range(4 if gathering else 2):
            if len(sends) > (50 if gathering else 24):
                sends.pop(0).wait_send()
    sum2 = l2_own[...]
    arrived(l2_recv, l2_r)
    for k in range(7):
        sum2 = sum2 + l2_recv[k]
    loss_out[0, 0] = 0.5 * jnp.sum(sum2)
    for cp in sends:
        cp.wait_send()


def shards(features, weight, norm_gain, target, counts):
    rows_g, depth = features.shape
    cols = weight.shape[1]
    total = target.shape[0]
    n = len(CHUNKS)
    bf, f32 = jnp.bfloat16, jnp.float32
    own = total // 16
    dma = pltpu.SemaphoreType.DMA
    anyspace = pl.BlockSpec(memory_space=pl.ANY)
    vmem = pl.BlockSpec(memory_space=pltpu.VMEM)
    unit = depth // 128
    a_units = unit * 14 // 24
    split = (a_units * 128, (a_units // 2) * 128, (unit // 2) * 128)
    out, loss = pl.pallas_call(
        functools.partial(kernel, cols * lax.axis_size("grp"), split),
        out_shape=(
            pltpu.VMEM((depth, cols), bf),
            jax.ShapeDtypeStruct((1, 1), f32),
        ),
        in_specs=[anyspace, anyspace, vmem, anyspace, pl.BlockSpec(memory_space=pltpu.SMEM), vmem],
        out_specs=(vmem, pl.BlockSpec(memory_space=pltpu.SMEM)),
        scratch_shapes=[
            pltpu.VMEM((total, depth), bf),
            pltpu.VMEM((depth, cols), bf),
            pltpu.VMEM((depth, cols), f32),
            pltpu.VMEM((total, cols), bf),
            pltpu.VMEM((total, cols), bf),
            pltpu.VMEM((total // 2, cols), bf),
            pltpu.VMEM((2, 8 * max(CHUNKS), cols), f32),
            pltpu.VMEM((total // 2, cols), bf),
            pltpu.VMEM((2, 3, own, cols), bf),
            pltpu.VMEM((own, cols), bf),
            pltpu.VMEM((own, cols), bf),
            pltpu.VMEM((own, cols), f32),
            pltpu.VMEM((own, cols), bf),
            pltpu.VMEM((n, 8, 128), f32),
            pltpu.VMEM((n, 7, 8, 128), f32),
            pltpu.VMEM((8, 128), f32),
            pltpu.VMEM((15, 8, 128), f32),
            pltpu.VMEM((8, 128), f32),
            pltpu.VMEM((7, 8, 128), f32),
            dma, dma((n,)), dma((n,)), dma((RING,)),
            dma((n, max(AG_SEM) + 1)), dma((n, 2)), dma((n, 2)), dma((n,)), dma((n,)), dma((n,)),
            dma((n, 6)), dma((n,)), dma, dma,
        ],
        compiler_params=pltpu.CompilerParams(
            collective_id=0, has_side_effects=True, vmem_limit_bytes=54 * 1024 * 1024
        ),
    )(features, weight, norm_gain.reshape(1, cols), target, counts, counts.reshape(2, -1))
    return out, loss[0, 0]


def solution(mesh):
    placed = (P("grp", "tp"), P("tp", "grp"), P("grp"), P(None, "grp"), P())
    return jax.shard_map(
        shards, mesh=mesh, in_specs=placed, out_specs=(P("tp", "grp"), P()), check_vma=False
    )
```
